32 devices in a mesh: groups: 2 (over x), seq: 16 (over z, y, core).
Axes of the slice: x: 2, y: 2, z: 4, core: 2. Of those that a mesh axis runs over, the one named last changes fastest.
Arguments:
- prefill_q: bfloat16 [32, 8192], P(('groups', 'seq')), parts along dimension 0, may hold values from -48 to 48
- cache_k: bfloat16 [16384, 1024], P(('groups', 'seq')), parts along dimension 0, may hold values from -4.5 to 4.5
- cache_v: bfloat16 [16384, 1024], P(('groups', 'seq')), parts along dimension 0, may hold values from -4.5 to 4.5
- page_counts: int32 [32], P('groups'), parts along dimension 0, may hold values from 1 to 64, 768 in all
- page_owner: int32 [2048, 1], P(('groups', 'seq')), parts along dimension 0, may hold values from 0 to 15; in each aligned block of 64 rows (0 to 63, 64 to 127, ...) at most 8 rows name the same one
- decode_q: bfloat16 [32, 2, 8192], P(('groups', 'seq')), parts along dimension 0, may hold values from -48 to 48
- decode_k: bfloat16 [32, 2, 1024], P(('groups', 'seq')), parts along dimension 0, may hold values from -12 to 12
- decode_v: bfloat16 [32, 2, 1024], P(('groups', 'seq')), parts along dimension 0, may hold values from -4.5 to 4.5
- context_len: int32 [32], P(('groups', 'seq')), parts along dimension 0, may hold values from 768 to 6144
Outputs:
- prefill_out: bfloat16 [32, 8192], P(('groups', 'seq')), parts along dimension 0
- decode_out: bfloat16 [32, 2, 8192], P(('groups', 'seq')), parts along dimension 0
- store_k: bfloat16 [32768, 1024], P(('groups', 'seq')), parts along dimension 0
- store_v: bfloat16 [32768, 1024], P(('groups', 'seq')), parts along dimension 0
- store_page: int32 [4096], P(('groups', 'seq')), parts along dimension 0
The draws below stay inside these ranges and needn't reach their ends.
There are 2 independent parts, one for each index of `groups`. The reference program is written for one: setup_inputs(seed, part) draws one part's arguments, and reference() takes and returns one part's arrays. A program takes and returns all parts, laid end to end along the dimension named above; each array names one. Nothing has to cross between parts.
Inputs may be any that keep to these rules, and one draw needn't show every extreme that they name: `page_counts`: the counts sum to 768 and the largest equals 64. `page_owner`: within the 64 page slots of one shard each owner is named at most 8 times, and exactly 8 times in some shards.
All inputs are finite; a program needn't handle non-finite values.
Results may differ from the reference program's by a relative error of at most 0.014.
Values may be sent and summed in bfloat16 or wider, within the bound.
A program may use at most 128 MiB of HBM per device.

```python
import math
import jax
import jax.numpy as jnp
import numpy as np
from jax import lax

HQ = 64
KVH = 8
HD = 128
PAGE = 8
PPD = 64
STEPS = 2
KVD = 1024
CAP = 8
TOTAL_PAGES = 768
SLOTS = 1024
STORE = 2048
SPAN = 16
REQ = 16
N_SEQ = 16


def shared_keys(key):
    base_key = jax.random.fold_in(key, 11)
    key_table = jnp.clip(jax.random.normal(base_key, (SLOTS * PAGE, KVD), jnp.float32), -4.5, 4.5)
    return key_table


def shared_queries(key, height, salt_value):
    base_key = jax.random.fold_in(key, salt_value)
    drawn_rows = jnp.clip(2.5 * jax.random.normal(base_key, (height, HQ * HD), jnp.float32), -15.0, 15.0)
    final_rows = drawn_rows
    return (drawn_rows, final_rows)


def draw_prefill_q(key, part):
    return shared_queries(key, SPAN, 31)[1].astype(jnp.bfloat16)


def draw_cache_k(key, part):
    return shared_keys(key).astype(jnp.bfloat16)


def draw_decode_q(key, part):
    return shared_queries(key, REQ * STEPS, 41)[1].reshape(REQ, STEPS, HQ * HD).astype(jnp.bfloat16)


def draw_decode_k(key, part):
    drawn_rows = shared_queries(key, REQ * STEPS, 41)[0]
    grouping = HQ // KVH
    summed = jnp.sum(drawn_rows.reshape(REQ * STEPS, KVH, grouping, HD), axis=2) * (0.5 / jnp.sqrt(jnp.float32(grouping)))
    noise_part = 0.5 * jax.random.normal(jax.random.fold_in(key, 51), (REQ * STEPS, KVH, HD), jnp.float32)
    return jnp.clip(summed + noise_part, -12.0, 12.0).reshape(REQ, STEPS, KVH * HD).astype(jnp.bfloat16)


def with_ends(values, key, smallest, largest):
    longest = values.shape.index(max(values.shape))
    spots = []
    for shift in (0, 1):
        where = [jax.random.randint(jax.random.fold_in(key, axis), (), 0, length) for axis, length in enumerate(values.shape)]
        where[longest] = (where[longest] + shift) % values.shape[longest]
        spots.append(tuple(where))
    return values.at[spots[0]].set(smallest).at[spots[1]].set(largest)


def level_of(stream_key, shape, pieces, least, largest):
    gain, own = 1.0, jax.random.fold_in(stream_key, 6)
    for dim, shards_of in pieces:
        heights = jnp.exp(jax.random.uniform(jax.random.fold_in(own, dim), (shards_of,), jnp.float32, least / len(pieces), largest / len(pieces)))
        gain = gain * jnp.repeat(heights, shape[dim] // shards_of).reshape([-1 if axis == dim else 1 for axis in range(len(shape))])
    return gain


def length_profile(amount, total, most, skew):
    portions = [(1 << 20) // math.isqrt(grade ** skew) + 1 for grade in range(2, amount + 1)]
    spare, holding = total - most - (amount - 1), [1] * (amount - 1)
    while spare > 0:
        movable = [i for i in range(amount - 1) if holding[i] < most]
        pool, remaining = sum([portions[i] for i in movable]), spare
        for i in movable:
            extra = min(most - holding[i], max(1, remaining * portions[i] // pool), spare)
            holding[i] = holding[i] + extra
            spare = spare - extra
    return np.array([most] + holding)


def ragged_sizes(rng, number_of, total, most, skew):
    if number_of == 2:
        one = jax.random.randint(rng, (), max(1, total - most), min(most, total - 1) + 1)
        return jnp.stack([one, total - one])
    lengths = jnp.asarray(length_profile(number_of, total, most, skew), jnp.int32)
    pairs = (number_of - 1) // 2
    giver, taker = lengths[1:1 + 2 * pairs:2], lengths[2:2 + 2 * pairs:2]
    slack = jnp.minimum(giver - 1, most - taker)
    moved = jax.random.randint(jax.random.fold_in(rng, 1), (pairs,), 0, 1 << 20) % (slack + 1)
    lengths = lengths.at[1:1 + 2 * pairs:2].set(giver - moved).at[2:2 + 2 * pairs:2].set(taker + moved)
    return lengths[jax.random.permutation(jax.random.fold_in(rng, 2), number_of)]


def shared_out(own_key, own, number, rows, number_of, top, bound, lean):
    order = jax.random.permutation(own_key, number_of)
    packed, usual = load_shares(number_of, rows * top, bound, lean, True), load_shares(number_of, rows * top, bound, lean, False)
    places = jnp.arange(number_of)

    def named(tallies, rotation):
        used = int((tallies > 0).sum())
        fixed = max(1, used // 4)
        moved = fixed + (places - fixed + rotation * (used - fixed)) % max(1, number_of - fixed)
        return jnp.zeros((number_of,), jnp.int32).at[order[jnp.where(places < fixed, places, moved)]].set(jnp.asarray(tallies, jnp.int32))

    tallies = jnp.where(number % 4 == 0, named(packed, number // 4), named(usual, number - number // 4 - 1))
    mixed = jax.random.permutation(jax.random.fold_in(own, 3), number_of)
    source_of, taker = mixed[0:number_of // 2 * 2:2], mixed[1:number_of // 2 * 2:2]
    room = jnp.minimum(tallies[source_of] - 1, bound - tallies[taker]) // 2
    room = jnp.where((source_of == order[0]) | (taker == order[0]) | (tallies[taker] == 0), 0, jnp.maximum(room, 0))
    moved = jax.random.randint(jax.random.fold_in(own, 4), (number_of // 2,), 0, 1 << 20) % (room + 1)
    tallies = tallies.at[source_of].add(-moved).at[taker].add(moved)
    members = jnp.searchsorted(jnp.cumsum(tallies), jnp.arange(rows * top), side="right").astype(jnp.int32)
    table = members.reshape(top, rows).T
    table = table[jax.random.permutation(jax.random.fold_in(own, 1), rows)]
    rotation = jax.random.randint(jax.random.fold_in(own, 2), (rows, 1), 0, top)
    return jnp.take_along_axis(table, (jnp.arange(top)[None, :] + rotation) % top, axis=1)


def load_shares(number_of, total, most, slope, full):
    portions = [(1 << 20) // math.isqrt(standing ** slope) + 1 for standing in range(1, number_of + 1)]
    largest = most if full else min(most, max(-(-total // number_of), total * portions[0] // sum(portions)))
    least = 1 if total - largest >= number_of - 1 else 0
    given, rest = [largest] + [least] * (number_of - 1), total - largest - least * (number_of - 1)
    while rest > 0:
        candidates = [i for i in range(1, number_of) if given[i] < largest] or [i for i in range(1, number_of) if given[i] < most]
        mass, left = sum([portions[i] for i in candidates]), rest
        for i in candidates:
            addition = min(most - given[i], max(1, left * portions[i] // mass), rest)
            given[i] = given[i] + addition
            rest = rest - addition
    return np.array(given)


def bell_draw(own_key, dims, spread, limit, shards=(), held_as=jnp.bfloat16):
    drawn = spread * jax.random.normal(own_key, dims, jnp.float32)
    if shards:
        drawn = drawn * level_of(own_key, dims, shards, -0.22, 0.18)
    return jnp.clip(drawn, -limit, limit).astype(held_as)


def setup_inputs(seed: int = 0, part: int = 0) -> dict:
    splits = jax.random.split(jax.random.key(seed), 10)
    part_keys = jax.random.split(jax.random.fold_in(splits[9], part), 10)
    prefill_q = draw_prefill_q(jax.random.fold_in(jax.random.fold_in(splits[9], part), 71), part)
    cache_k = draw_cache_k(jax.random.fold_in(jax.random.fold_in(splits[9], part), 71), part)
    cache_v = bell_draw(part_keys[2], (SLOTS * PAGE, KVD), 1.0, 4.5, ((0, 16),))
    page_counts = ragged_sizes(part_keys[3], N_SEQ, TOTAL_PAGES, PPD, 2).astype(jnp.int32)
    page_owner_keys = jax.random.split(jax.random.fold_in(part_keys[4], 1), SLOTS // PPD)
    page_owner_turns = jax.random.permutation(jax.random.fold_in(part_keys[4], 3), SLOTS // PPD)
    page_owner = jax.vmap(lambda own, number: shared_out(jax.random.fold_in(part_keys[4], 2), own, number, PPD, N_SEQ, 1, CAP, 2))(page_owner_keys, page_owner_turns).reshape((SLOTS, 1))
    decode_q = draw_decode_q(jax.random.fold_in(jax.random.fold_in(splits[9], part), 71), part)
    decode_k = draw_decode_k(jax.random.fold_in(jax.random.fold_in(splits[9], part), 71), part)
    decode_v = bell_draw(part_keys[7], (REQ, STEPS, KVD), 1.0, 4.5, ((0, 16),))
    context_len = with_ends(jax.random.randint(part_keys[8], (REQ,), PAGE * TOTAL_PAGES // 8, PAGE * TOTAL_PAGES + 1), jax.random.fold_in(part_keys[8], 1), PAGE * TOTAL_PAGES // 8, PAGE * TOTAL_PAGES).astype(jnp.int32)
    return dict(prefill_q=prefill_q, cache_k=cache_k, cache_v=cache_v, page_counts=page_counts, page_owner=page_owner, decode_q=decode_q, decode_k=decode_k, decode_v=decode_v, context_len=context_len)


MASKED = -1.0e30
EXACT = lax.Precision.HIGHEST


def attention(queries, key_block, value_block, allowed, own_keys, own_values, own_allowed):
    height = queries.shape[0]
    grouping = HQ // KVH
    scaling = HD ** -0.5
    query_all = queries.astype(jnp.float32).reshape(height, KVH, grouping, HD)
    key_all = key_block.astype(jnp.float32).reshape(-1, KVH, HD)
    value_all = value_block.astype(jnp.float32).reshape(-1, KVH, HD)
    if own_keys is not None:
        own_key_all = own_keys.astype(jnp.float32).reshape(height, -1, KVH, HD)
        own_value_all = own_values.astype(jnp.float32).reshape(height, -1, KVH, HD)

    def per_group(member):
        query_group = lax.dynamic_index_in_dim(query_all, member, 1, keepdims=False)
        key_group = lax.dynamic_index_in_dim(key_all, member, 1, keepdims=False)
        value_group = lax.dynamic_index_in_dim(value_all, member, 1, keepdims=False)
        scores = jnp.einsum("qhd,kd->qhk", query_group, key_group, precision=EXACT) * scaling
        scores = jnp.where(allowed[:, None, :], scores, MASKED)
        highest = jnp.max(scores, axis=2)
        if own_keys is not None:
            own_key_group = lax.dynamic_index_in_dim(own_key_all, member, 2, keepdims=False)
            own_value_group = lax.dynamic_index_in_dim(own_value_all, member, 2, keepdims=False)
            own_scores = jnp.einsum("qhd,qtd->qht", query_group, own_key_group, precision=EXACT) * scaling
            own_scores = jnp.where(own_allowed[:, None, :], own_scores, MASKED)
            highest = jnp.maximum(highest, jnp.max(own_scores, axis=2))
        weights = jnp.where(allowed[:, None, :], jnp.exp(scores - highest[:, :, None]), 0.0)
        totals = jnp.sum(weights, axis=2)
        if own_keys is not None:
            own_weights = jnp.where(own_allowed[:, None, :], jnp.exp(own_scores - highest[:, :, None]), 0.0)
            totals = totals + jnp.sum(own_weights, axis=2)
        probs = lax.optimization_barrier((weights / totals[:, :, None]).astype(jnp.bfloat16)).astype(jnp.float32)
        result = jnp.einsum("qhk,kd->qhd", probs, value_group, precision=EXACT)
        if own_keys is not None:
            own_probs = lax.optimization_barrier((own_weights / totals[:, :, None]).astype(jnp.bfloat16)).astype(jnp.float32)
            result = result + jnp.einsum("qht,qtd->qhd", own_probs, own_value_group, precision=EXACT)
        return result

    outputs = lax.map(per_group, jnp.arange(KVH, dtype=jnp.int32))
    return outputs.transpose(1, 0, 2, 3).reshape(height, HQ * HD).astype(jnp.bfloat16)


def reference(prefill_q, cache_k, cache_v, page_counts, page_owner, decode_q, decode_k, decode_v, context_len):
    shard_rows = PPD * PAGE
    key_rows = jnp.arange(SLOTS * PAGE, dtype=jnp.int32)
    device_of = key_rows // shard_rows
    local_row = key_rows % shard_rows
    before = (jnp.cumsum(page_counts) - page_counts).astype(jnp.int32)
    usable = local_row < PAGE * page_counts[device_of]
    places = PAGE * before[device_of] + local_row
    prompt = PAGE * jnp.sum(page_counts).astype(jnp.int32)
    query_places = prompt - SPAN + jnp.arange(SPAN, dtype=jnp.int32)
    allowed = usable[None, :] & (places[None, :] <= query_places[:, None])
    prefill_out = attention(prefill_q, cache_k, cache_v, allowed, None, None, None)

    query_rows = decode_q.reshape(REQ * STEPS, HQ * HD)
    limits = jnp.repeat(context_len, STEPS)
    decode_allowed = usable[None, :] & (places[None, :] < limits[:, None])
    own_keys = jnp.repeat(decode_k, STEPS, axis=0)
    own_values = jnp.repeat(decode_v, STEPS, axis=0)
    steps_now = jnp.tile(jnp.arange(STEPS, dtype=jnp.int32), REQ)
    own_allowed = jnp.arange(STEPS, dtype=jnp.int32)[None, :] <= steps_now[:, None]
    decode_out = attention(query_rows, cache_k, cache_v, decode_allowed, own_keys, own_values, own_allowed)
    decode_out = decode_out.reshape(REQ, STEPS, HQ * HD)

    owners = page_owner[:, 0]
    page_index = jnp.arange(SLOTS, dtype=jnp.int32)
    page_device = page_index // PPD
    page_live = (page_index % PPD) < page_counts[page_device]
    chosen = owners[:, None] == jnp.arange(N_SEQ, dtype=jnp.int32)[None, :]
    chosen_live = (chosen & page_live[:, None]).astype(jnp.int32).reshape(N_SEQ, PPD, N_SEQ)
    earlier = (jnp.cumsum(chosen_live, axis=1) - chosen_live).astype(jnp.int32).reshape(SLOTS, N_SEQ)
    ranking = jnp.sum(earlier * chosen.astype(jnp.int32), axis=1).astype(jnp.int32)
    target = jnp.where(page_live, owners * (N_SEQ * CAP) + page_device * CAP + ranking, STORE).astype(jnp.int32)
    store_k = jnp.zeros((STORE, PAGE * KVD), cache_k.dtype).at[target].set(cache_k.reshape(SLOTS, PAGE * KVD), mode="drop")
    store_v = jnp.zeros((STORE, PAGE * KVD), cache_v.dtype).at[target].set(cache_v.reshape(SLOTS, PAGE * KVD), mode="drop")
    store_page = jnp.full((STORE,), -1, jnp.int32).at[target].set(page_index, mode="drop")
    return prefill_out, decode_out, store_k.reshape(STORE * PAGE, KVD), store_v.reshape(STORE * PAGE, KVD), store_page
```

```python
import functools

import jax
import jax.numpy as jnp
from jax import lax
from jax.experimental import pallas as pl
from jax.experimental.pallas import tpu as pltpu
from jax.sharding import PartitionSpec as P

HQ = 64
KVH = 8
HD = 128
PAGE = 8
STEPS = 2
KVD = 1024
GROUP = HQ // KVH
ROWS = (1 + STEPS) * GROUP
LANES = 128
ID_LANE = 64
MASKED = -1e30
SCALE = HD ** (-0.5)
MESH = pl.DeviceIdType.MESH

Q, META, KEYS, VALUES, PART, STAT = range(6)


def pack_kernel(n, cap, page_slots, owner, counts, context, ck, cv, out_k, out_v, meta, table, seen):
    dst = pl.program_id(0)
    me = lax.axis_index("seq")

    @pl.when(dst == 0)
    def _():
        def clear(i, _):
            table[i] = -1
            return 0

        lax.fori_loop(0, n * cap, clear, 0)

        def clear_seen(i, _):
            seen[i] = 0
            return 0

        lax.fori_loop(0, n, clear_seen, 0)

        def place(j, _):
            o = owner[j]
            k = seen[o]
            seen[o] = k + 1
            table[o * cap + k] = j
            return 0

        lax.fori_loop(0, counts[me], place, 0)

    tile_row = lax.broadcasted_iota(jnp.int32, (8, LANES), 0)
    ids = jnp.full((8, LANES), -1, jnp.int32)
    for k in range(cap):
        src = table[dst * cap + k]
        ids = jnp.where(tile_row == k, jnp.where(src >= 0, me * page_slots + src, -1), ids)

        @pl.when(src >= 0)
        def _():
            out_k[k] = ck[src]
            out_v[k] = cv[src]

        @pl.when(src < 0)
        def _():
            out_k[k] = jnp.zeros((PAGE, KVD), out_k.dtype)
            out_v[k] = jnp.zeros((PAGE, KVD), out_v.dtype)

    lane = lax.broadcasted_iota(jnp.int32, (8, LANES), 1)
    meta[0] = jnp.where(lane < ID_LANE, context[0], ids)


def pack(n, cap, owner, counts, context, ck, cv):
    page_slots = ck.shape[0]
    smem = pl.BlockSpec(memory_space=pltpu.SMEM)
    whole = pl.BlockSpec(ck.shape, lambda d: (0, 0, 0))
    block = pl.BlockSpec((cap, PAGE, KVD), lambda d: (d, 0, 0))
    return pl.pallas_call(
        functools.partial(pack_kernel, n, cap, page_slots),
        grid=(n,),
        in_specs=[smem, smem, smem, whole, whole],
        out_specs=(block, block, pl.BlockSpec((1, 8, LANES), lambda d: (d, 0, 0))),
        out_shape=(
            jax.ShapeDtypeStruct((n * cap, PAGE, KVD), ck.dtype),
            jax.ShapeDtypeStruct((n * cap, PAGE, KVD), cv.dtype),
            jax.ShapeDtypeStruct((n, 8, LANES), jnp.int32),
        ),
        scratch_shapes=[pltpu.SMEM((n * cap,), jnp.int32), pltpu.SMEM((n,), jnp.int32)],
        name="pack",
    )(owner, counts, context, ck, cv)


def main_kernel(
    n, cap, chunk, bounds, q_ref, meta_ref, ck_ref, cv_ref, pk_ref, pv_ref, ok_ref, ov_ref,
    out_ref, store_k, store_v, meta_out,
    qbuf, obuf, stat, limit, pbuf, sbuf, send, recv, local,
):
    me = lax.axis_index("seq")

    def rows_of(d):
        return pl.ds(pl.multiple_of(d * ROWS, 8), ROWS)

    def slots_of(d):
        return pl.ds(d * cap, cap)

    def ends(kind, peer, writer):
        if kind == Q:
            return q_ref, qbuf.at[:, rows_of(writer), :]
        if kind == META:
            return meta_ref.at[peer], meta_out.at[writer]
        if kind == KEYS:
            return pk_ref.at[slots_of(peer)], store_k.at[slots_of(writer)]
        if kind == VALUES:
            return pv_ref.at[slots_of(peer)], store_v.at[slots_of(writer)]
        if kind == PART:
            return obuf.at[:, rows_of(peer), :], pbuf.at[writer]
        return stat.at[rows_of(peer), :], sbuf.at[writer]

    def outgoing(kind, peer):
        src, dst = ends(kind, peer, me)
        return pltpu.make_async_remote_copy(
            src_ref=src, dst_ref=dst, send_sem=send.at[kind, peer], recv_sem=recv.at[kind, me],
            device_id={"seq": peer}, device_id_type=MESH,
        )

    def incoming(kind, peer):
        src, dst = ends(kind, peer, peer)
        return pltpu.make_async_remote_copy(
            src_ref=src, dst_ref=dst, send_sem=send.at[kind, peer], recv_sem=recv.at[kind, peer],
            device_id={"seq": peer}, device_id_type=MESH,
        )

    def own(kind):
        src, dst = ends(kind, me, me)
        return pltpu.make_async_copy(src, dst, local.at[kind])

    def each_peer(body):
        def step(i, _):
            body(lax.rem(me + i, n))
            return 0

        lax.fori_loop(1, n, step, 0)

    barrier = pltpu.get_barrier_semaphore()
    each_peer(
        lambda peer: pl.semaphore_signal(
            barrier, inc=1, device_id={"seq": peer}, device_id_type=MESH
        )
    )
    pl.semaphore_wait(barrier, n - 1)

    def start_small(peer):
        outgoing(META, peer).start()
        outgoing(Q, peer).start()

    def start_pages(peer):
        outgoing(KEYS, peer).start()
        outgoing(VALUES, peer).start()

    each_peer(start_small)
    for kind in (META, Q, KEYS, VALUES):
        own(kind).start()
    each_peer(start_pages)

    own(META).wait()
    own(Q).wait()

    def wait_small(peer):
        incoming(META, peer).wait_recv()
        incoming(Q, peer).wait_recv()

    each_peer(wait_small)

    live, start, first = bounds[0], bounds[1], bounds[2]

    def set_limit(d, _):
        base = pl.multiple_of(d * ROWS, 8)
        context = jnp.broadcast_to(meta_out[d][:, 0:1], (8, LANES))
        reach = jnp.minimum(live, context - start)
        limit[pl.ds(base, 8), :] = jnp.full((8, LANES), jnp.minimum(live, first + d + 1 - start))
        for s in range(STEPS):
            limit[pl.ds(pl.multiple_of(base + 8 * (s + 1), 8), 8), :] = reach
        return 0

    lax.fori_loop(0, n, set_limit, 0)

    lane = lax.broadcasted_iota(jnp.int32, (chunk, LANES), 1)
    keys = ck_ref.shape[0]

    def attend(c, _):
        rows = pl.ds(pl.multiple_of(c * chunk, 16), chunk)

        def head(g, stats):
            cols = pl.ds(pl.multiple_of(g * HD, HD), HD)
            scores = lax.dot_general(
                qbuf[g, rows, :], ck_ref[:, cols], (((1,), (1,)), ((), ())),
                preferred_element_type=jnp.float32,
            ) * SCALE
            place = lax.broadcasted_iota(jnp.int32, (chunk, keys), 1)
            bound = limit[rows, 0:1]
            scores = jnp.where(place < bound, scores, MASKED)
            high = jnp.max(scores, axis=1, keepdims=True)
            weights = jnp.exp(scores - high)
            total = jnp.sum(weights, axis=1, keepdims=True)
            summed = jnp.dot(
                weights.astype(jnp.bfloat16), cv_ref[:, cols], preferred_element_type=jnp.float32
            )
            obuf[g, rows, :] = (summed / total).astype(jnp.bfloat16)
            level = jnp.where(bound > 0, high + jnp.log(total), MASKED)
            return jnp.where(lane == g, level, stats)

        stat[rows, :] = lax.fori_loop(0, KVH, head, jnp.zeros((chunk, LANES), jnp.float32))
        return 0

    lax.fori_loop(0, stat.shape[0] // chunk, attend, 0)

    def start_parts(peer):
        outgoing(STAT, peer).start()
        outgoing(PART, peer).start()

    each_peer(start_parts)
    own(STAT).start()
    own(PART).start()

    own_lane = lax.broadcasted_iota(jnp.int32, (ROWS, LANES), 1)
    own_row = lax.broadcasted_iota(jnp.int32, (ROWS, LANES), 0)
    own_levels = []
    for t in range(STEPS):
        level = jnp.zeros((ROWS, LANES), jnp.float32)
        for g in range(KVH):
            key = ok_ref[t : t + 1, g * HD : (g + 1) * HD].astype(jnp.float32)
            score = jnp.sum(q_ref[g].astype(jnp.float32) * key, axis=1, keepdims=True) * SCALE
            level = jnp.where(own_lane == g, score, level)
        own_levels.append(jnp.where(own_row >= GROUP * (t + 1), level, MASKED))

    own(STAT).wait()
    own(PART).wait()

    def wait_parts(peer):
        incoming(STAT, peer).wait_recv()
        incoming(PART, peer).wait_recv()

    each_peer(wait_parts)

    top = functools.reduce(jnp.maximum, own_levels)
    top = lax.fori_loop(0, n, lambda d, high: jnp.maximum(high, sbuf[d]), top)

    norm = jnp.zeros((ROWS, LANES), jnp.float32)
    sums = [jnp.zeros((ROWS, HD), jnp.float32) for _ in range(KVH)]
    for t in range(STEPS):
        factor = jnp.exp(own_levels[t] - top)
        norm = norm + factor
        for g in range(KVH):
            value = ov_ref[t : t + 1, g * HD : (g + 1) * HD].astype(jnp.float32)
            sums[g] = sums[g] + factor[:, g : g + 1] * value

    def add(d, state):
        norm, sums = state
        factor = jnp.exp(sbuf[d] - top)
        sums = tuple(
            sums[g] + factor[:, g : g + 1] * pbuf[d, g].astype(jnp.float32) for g in range(KVH)
        )
        return norm + factor, sums

    norm, sums = lax.fori_loop(0, n, add, (norm, tuple(sums)))
    for g in range(KVH):
        out_ref[g] = (sums[g] / norm[:, g : g + 1]).astype(out_ref.dtype)

    own(KEYS).wait()
    own(VALUES).wait()

    def finish(peer):
        incoming(KEYS, peer).wait_recv()
        incoming(VALUES, peer).wait_recv()
        for kind in (Q, META, KEYS, VALUES, PART, STAT):
            outgoing(kind, peer).wait_send()

    each_peer(finish)


def main(n, cap, bounds, q, meta, ck, cv, pk, pv, own_k, own_v):
    height = n * ROWS
    chunk = min(height, 384)
    vmem = pl.BlockSpec(memory_space=pltpu.VMEM)
    smem = pl.BlockSpec(memory_space=pltpu.SMEM)
    hbm = pl.BlockSpec(memory_space=pl.ANY)
    return pl.pallas_call(
        functools.partial(main_kernel, n, cap, chunk),
        in_specs=[smem, vmem, vmem, vmem, vmem, hbm, hbm, vmem, vmem],
        out_specs=(vmem, hbm, hbm, vmem),
        out_shape=(
            jax.ShapeDtypeStruct((KVH, ROWS, HD), jnp.bfloat16),
            jax.ShapeDtypeStruct(pk.shape, pk.dtype),
            jax.ShapeDtypeStruct(pv.shape, pv.dtype),
            jax.ShapeDtypeStruct(meta.shape, meta.dtype),
        ),
        scratch_shapes=[
            pltpu.VMEM((KVH, height, HD), jnp.bfloat16),
            pltpu.VMEM((KVH, height, HD), jnp.bfloat16),
            pltpu.VMEM((height, LANES), jnp.float32),
            pltpu.VMEM((height, LANES), jnp.int32),
            pltpu.VMEM((n, KVH, ROWS, HD), jnp.bfloat16),
            pltpu.VMEM((n, ROWS, LANES), jnp.float32),
            pltpu.SemaphoreType.DMA((6, n)),
            pltpu.SemaphoreType.DMA((6, n)),
            pltpu.SemaphoreType.DMA((6,)),
        ],
        compiler_params=pltpu.CompilerParams(
            collective_id=0, has_side_effects=True, vmem_limit_bytes=48 << 20
        ),
        name="exchange",
    )(bounds, q, meta, ck, cv, pk, pv, own_k, own_v)


def per_device(
    prefill_q, cache_k, cache_v, page_counts, page_owner, decode_q, decode_k, decode_v, context_len
):
    n = lax.axis_size("seq")
    me = lax.axis_index("seq")
    page_slots = cache_k.shape[0] // PAGE
    cap = max(2, 2 * page_slots // n)
    ck = cache_k.reshape(page_slots, PAGE, KVD)
    cv = cache_v.reshape(page_slots, PAGE, KVD)
    pk, pv, meta = pack(n, cap, page_owner[:, 0], page_counts, context_len, ck, cv)
    position = jnp.arange(n, dtype=jnp.int32)
    bounds = PAGE * jnp.stack(
        [
            jnp.sum(jnp.where(position == me, page_counts, 0)),
            jnp.sum(jnp.where(position < me, page_counts, 0)),
            jnp.sum(page_counts),
        ]
    ) - jnp.array([0, 0, n], jnp.int32)
    q = jnp.concatenate((prefill_q, decode_q[0]), axis=0)
    q = q.reshape(1 + STEPS, KVH, GROUP, HD).transpose(1, 0, 2, 3).reshape(KVH, ROWS, HD)
    out, store_k, store_v, meta = main(
        n, cap, bounds, q, meta, cache_k, cache_v, pk, pv, decode_k[0], decode_v[0]
    )
    out = out.reshape(KVH, 1 + STEPS, GROUP, HD).transpose(1, 0, 2, 3).reshape(1 + STEPS, HQ * HD)
    return (
        out[:1],
        out[1:].reshape(1, STEPS, HQ * HD),
        store_k.reshape(-1, KVD),
        store_v.reshape(-1, KVD),
        meta[:, :cap, ID_LANE].reshape(-1),
    )


def solution(mesh):
    both = ("groups", "seq")
    in_specs = (
        P(both, None),
        P(both, None),
        P(both, None),
        P("groups"),
        P(both, None),
        P(both, None, None),
        P(both, None, None),
        P(both, None, None),
        P(both),
    )
    out_specs = (
        P(both, None),
        P(both, None, None),
        P(both, None),
        P(both, None),
        P(both),
    )
    return jax.shard_map(
        per_device, mesh=mesh, in_specs=in_specs, out_specs=out_specs, check_vma=False
    )
```

```python
import functools

import jax
import jax.numpy as jnp
from jax import lax
from jax.experimental import pallas as pl
from jax.experimental.pallas import tpu as pltpu
from jax.sharding import PartitionSpec as P

HQ = 64
KVH = 8
HD = 128
PAGE = 8
STEPS = 2
KVD = 1024
GROUP = HQ // KVH
ROWS = (1 + STEPS) * GROUP
LANES = 128
ID_LANE = 64
MASKED = -1e30
SCALE = HD ** (-0.5)
MESH = pl.DeviceIdType.MESH

META, KEYS, VALUES = range(3)
QROW, PART, STAT = range(3)


def pack_kernel(n, cap, page_slots, owner, counts, context, ck, cv, out_k, out_v, meta, table, seen):
    dst = pl.program_id(0)
    me = lax.axis_index("seq")

    @pl.when(dst == 0)
    def _():
        def clear(i, _):
            table[i] = -1
            return 0

        lax.fori_loop(0, n * cap, clear, 0)

        def clear_seen(i, _):
            seen[i] = 0
            return 0

        lax.fori_loop(0, n, clear_seen, 0)

        def place(j, _):
            o = owner[j]
            k = seen[o]
            seen[o] = k + 1
            table[o * cap + k] = j
            return 0

        lax.fori_loop(0, counts[me], place, 0)

    tile_row = lax.broadcasted_iota(jnp.int32, (8, LANES), 0)
    ids = jnp.full((8, LANES), -1, jnp.int32)
    for k in range(cap):
        src = table[dst * cap + k]
        ids = jnp.where(tile_row == k, jnp.where(src >= 0, me * page_slots + src, -1), ids)

        @pl.when(src >= 0)
        def _():
            out_k[k] = ck[src]
            out_v[k] = cv[src]

        @pl.when(src < 0)
        def _():
            out_k[k] = jnp.zeros((PAGE, KVD), out_k.dtype)
            out_v[k] = jnp.zeros((PAGE, KVD), out_v.dtype)

    lane = lax.broadcasted_iota(jnp.int32, (8, LANES), 1)
    meta[0] = jnp.where(lane < ID_LANE, context[0], ids)


def pack(n, cap, owner, counts, context, ck, cv):
    page_slots = ck.shape[0]
    smem = pl.BlockSpec(memory_space=pltpu.SMEM)
    whole = pl.BlockSpec(ck.shape, lambda d: (0, 0, 0))
    block = pl.BlockSpec((cap, PAGE, KVD), lambda d: (d, 0, 0))
    return pl.pallas_call(
        functools.partial(pack_kernel, n, cap, page_slots),
        grid=(n,),
        in_specs=[smem, smem, smem, whole, whole],
        out_specs=(block, block, pl.BlockSpec((1, 8, LANES), lambda d: (d, 0, 0))),
        out_shape=(
            jax.ShapeDtypeStruct((n * cap, PAGE, KVD), ck.dtype),
            jax.ShapeDtypeStruct((n * cap, PAGE, KVD), cv.dtype),
            jax.ShapeDtypeStruct((n, 8, LANES), jnp.int32),
        ),
        scratch_shapes=[pltpu.SMEM((n * cap,), jnp.int32), pltpu.SMEM((n,), jnp.int32)],
        name="pack",
    )(owner, counts, context, ck, cv)


def main_kernel(
    n, cap, chunk, counts, q_ref, meta_ref, ck_ref, cv_ref, pk_ref, pv_ref, ok_ref, ov_ref,
    out_ref, store_k, store_v, meta_out,
    qbuf, obuf, stat, limit, got1, got1s, obuf1, stat1, got2, got2s, obuf2, stat2, pbuf, sbuf,
    page_send, page_recv, row_send, row_recv, pair_send, pair_recv, local,
):
    depth = n // 4
    me = lax.axis_index("seq")
    my_z, my_y, my_c = me // 4, (me // 2) % 2, me % 2
    block = (my_c * 2 + my_y) * depth + my_z
    across = my_z * 4 + (1 - my_y) * 2 + my_c
    sibling = my_z * 4 + my_y * 2 + (1 - my_c)

    def rows_of(first, count=1):
        return pl.ds(pl.multiple_of(first * ROWS, 8), count * ROWS)

    def slots_of(d):
        return pl.ds(d * cap, cap)

    def page_ends(kind, peer, writer):
        if kind == META:
            return meta_ref.at[peer], meta_out.at[writer]
        if kind == KEYS:
            return pk_ref.at[slots_of(peer)], store_k.at[slots_of(writer)]
        return pv_ref.at[slots_of(peer)], store_v.at[slots_of(writer)]

    def page(kind, peer, arriving=False):
        src, dst = page_ends(kind, peer, peer if arriving else me)
        return pltpu.make_async_remote_copy(
            src_ref=src, dst_ref=dst, send_sem=page_send.at[kind, peer],
            recv_sem=page_recv.at[kind, peer if arriving else me],
            device_id={"seq": peer}, device_id_type=MESH,
        )

    def row_ends(kind, z, writer):
        if kind == QROW:
            return q_ref, qbuf.at[:, rows_of((my_c * 2 + my_y) * depth + writer), :]
        if kind == PART:
            return obuf2.at[:, rows_of(z), :], pbuf.at[writer]
        return stat2.at[rows_of(z), :], sbuf.at[writer]

    def row(kind, z, arriving=False):
        src, dst = row_ends(kind, z, z if arriving else my_z)
        return pltpu.make_async_remote_copy(
            src_ref=src, dst_ref=dst, send_sem=row_send.at[kind, z],
            recv_sem=row_recv.at[kind, z if arriving else my_z],
            device_id={"seq": z * 4 + my_y * 2 + my_c}, device_id_type=MESH,
        )

    def pair(number, src, dst, peer):
        return pltpu.make_async_remote_copy(
            src_ref=src, dst_ref=dst, send_sem=pair_send.at[number], recv_sem=pair_recv.at[number],
            device_id={"seq": peer}, device_id_type=MESH,
        )

    def own_page(kind):
        src, dst = page_ends(kind, me, me)
        return pltpu.make_async_copy(src, dst, local.at[kind])

    def own_row(kind):
        src, dst = row_ends(kind, my_z, my_z)
        return pltpu.make_async_copy(src, dst, local.at[3 + kind])

    def each(count, mine, body):
        def step(i, _):
            body(lax.rem(mine + i, count))
            return 0

        lax.fori_loop(1, count, step, 0)

    barrier = pltpu.get_barrier_semaphore()

    def greet(peer):
        pl.semaphore_signal(barrier, inc=1, device_id={"seq": peer}, device_id_type=MESH)

    each(n, me, greet)
    pl.semaphore_wait(barrier, n - 1)

    each(depth, my_z, lambda z: row(QROW, z).start())
    own_row(QROW).start()
    each(n, me, lambda peer: page(META, peer).start())
    for kind in (META, KEYS, VALUES):
        own_page(kind).start()

    def start_pages(peer):
        page(KEYS, peer).start()
        page(VALUES, peer).start()

    def near(i, _):
        z = lax.rem(my_z + depth // 2 + i, depth)

        @pl.when(z != my_z)
        def _():
            start_pages(z * 4 + my_y * 2 + my_c)
            start_pages(z * 4 + my_y * 2 + (1 - my_c))

        return 0

    lax.fori_loop(0, depth, near, 0)

    own_row(QROW).wait()
    each(depth, my_z, lambda z: row(QROW, z, True).wait_recv())
    q_y_out = qbuf.at[:, rows_of((my_c * 2 + my_y) * depth, depth), :]
    q_y_in = qbuf.at[:, rows_of((my_c * 2 + 1 - my_y) * depth, depth), :]
    pair(0, q_y_out, q_y_out, across).start()
    pair(0, q_y_out, q_y_in, across).wait_recv()
    q_c_out = qbuf.at[:, rows_of(my_c * 2 * depth, 2 * depth), :]
    q_c_in = qbuf.at[:, rows_of((1 - my_c) * 2 * depth, 2 * depth), :]
    pair(1, q_c_out, q_c_out, sibling).start()
    own_page(META).wait()
    each(n, me, lambda peer: page(META, peer, True).wait_recv())

    live = PAGE * counts[me]
    start = PAGE * lax.fori_loop(
        0, n, lambda i, sofar: sofar + jnp.where(i < me, counts[i], 0), jnp.int32(0)
    )
    prompt = PAGE * lax.fori_loop(0, n, lambda i, sofar: sofar + counts[i], jnp.int32(0))

    def set_limit(p, _):
        d = (p % depth) * 4 + ((p // depth) % 2) * 2 + p // (2 * depth)
        base = pl.multiple_of(p * ROWS, 8)
        context = jnp.broadcast_to(meta_out[d][:, 0:1], (8, LANES))
        reach = jnp.minimum(live, context - start)
        limit[pl.ds(base, 8), :] = jnp.full(
            (8, LANES), jnp.minimum(live, prompt - n + d + 1 - start)
        )
        for s in range(STEPS):
            limit[pl.ds(pl.multiple_of(base + 8 * (s + 1), 8), 8), :] = reach
        return 0

    lax.fori_loop(0, n, set_limit, 0)
    pair(1, q_c_out, q_c_in, sibling).wait_recv()

    lane = lax.broadcasted_iota(jnp.int32, (chunk, LANES), 1)
    keys = ck_ref.shape[0]

    def attend(c, _):
        rows = pl.ds(pl.multiple_of(c * chunk, 16), chunk)

        def head(g, stats):
            cols = pl.ds(pl.multiple_of(g * HD, HD), HD)
            scores = lax.dot_general(
                qbuf[g, rows, :], ck_ref[:, cols], (((1,), (1,)), ((), ())),
                preferred_element_type=jnp.float32,
            ) * SCALE
            place = lax.broadcasted_iota(jnp.int32, (chunk, keys), 1)
            bound = limit[rows, 0:1]
            scores = jnp.where(place < bound, scores, MASKED)
            high = jnp.max(scores, axis=1, keepdims=True)
            weights = jnp.exp(scores - high)
            total = jnp.sum(weights, axis=1, keepdims=True)
            summed = jnp.dot(
                weights.astype(jnp.bfloat16), cv_ref[:, cols], preferred_element_type=jnp.float32
            )
            obuf[g, rows, :] = (summed / total).astype(jnp.bfloat16)
            level = jnp.where(bound > 0, high + jnp.log(total), MASKED)
            return jnp.where(lane == g, level, stats)

        stat[rows, :] = lax.fori_loop(0, KVH, head, jnp.zeros((chunk, LANES), jnp.float32))
        return 0

    lax.fori_loop(0, stat.shape[0] // chunk, attend, 0)

    def merge(a, a_stat, first, b, b_stat, to, to_stat):
        step = 2 * ROWS

        def some(i, _):
            here = pl.ds(pl.multiple_of(i * step, 16), step)
            there = pl.ds(pl.multiple_of(first * ROWS + i * step, 16), step)
            one, two = a_stat[there, :], b_stat[here, :]
            high = jnp.maximum(one, two)
            one, two = jnp.exp(one - high), jnp.exp(two - high)
            both = one + two
            to_stat[here, :] = high + jnp.log(both)
            one, two = one / both, two / both
            for g in range(KVH):
                to[g, here, :] = (
                    one[:, g : g + 1] * a[g, there, :].astype(jnp.float32)
                    + two[:, g : g + 1] * b[g, here, :].astype(jnp.float32)
                ).astype(jnp.bfloat16)
            return 0

        lax.fori_loop(0, to_stat.shape[0] // step, some, 0)

    give = (1 - my_c) * 2 * depth
    part1 = pair(2, obuf.at[:, rows_of(give, 2 * depth), :], got1, sibling)
    part1s = pair(3, stat.at[rows_of(give, 2 * depth), :], got1s, sibling)
    part1s.start()
    part1.start()
    part1s.wait_recv()
    part1.wait_recv()
    merge(obuf, stat, my_c * 2 * depth, got1, got1s, obuf1, stat1)
    give = (1 - my_y) * depth
    part2 = pair(4, obuf1.at[:, rows_of(give, depth), :], got2, across)
    part2s = pair(5, stat1.at[rows_of(give, depth), :], got2s, across)
    part2s.start()
    part2.start()
    start_pages(sibling)

    own_lane = lax.broadcasted_iota(jnp.int32, (ROWS, LANES), 1)
    own_place = lax.broadcasted_iota(jnp.int32, (ROWS, LANES), 0)
    own_levels = []
    for t in range(STEPS):
        level = jnp.zeros((ROWS, LANES), jnp.float32)
        for g in range(KVH):
            key = ok_ref[t : t + 1, g * HD : (g + 1) * HD].astype(jnp.float32)
            score = jnp.sum(q_ref[g].astype(jnp.float32) * key, axis=1, keepdims=True) * SCALE
            level = jnp.where(own_lane == g, score, level)
        own_levels.append(jnp.where(own_place >= GROUP * (t + 1), level, MASKED))

    part2s.wait_recv()
    part2.wait_recv()
    merge(obuf1, stat1, my_y * depth, got2, got2s, obuf2, stat2)

    def start_rows(z):
        row(STAT, z).start()
        row(PART, z).start()

    each(depth, my_z, start_rows)
    own_row(STAT).start()
    own_row(PART).start()

    def far(i, _):
        z = lax.rem(my_z + depth // 2 + i, depth)
        start_pages(z * 4 + (1 - my_y) * 2 + my_c)
        start_pages(z * 4 + (1 - my_y) * 2 + (1 - my_c))
        return 0

    lax.fori_loop(0, depth, far, 0)

    own_row(STAT).wait()
    own_row(PART).wait()

    def wait_rows(z):
        row(STAT, z, True).wait_recv()
        row(PART, z, True).wait_recv()

    each(depth, my_z, wait_rows)

    top = functools.reduce(jnp.maximum, own_levels)
    top = lax.fori_loop(0, depth, lambda d, high: jnp.maximum(high, sbuf[d]), top)

    norm = jnp.zeros((ROWS, LANES), jnp.float32)
    sums = [jnp.zeros((ROWS, HD), jnp.float32) for _ in range(KVH)]
    for t in range(STEPS):
        factor = jnp.exp(own_levels[t] - top)
        norm = norm + factor
        for g in range(KVH):
            value = ov_ref[t : t + 1, g * HD : (g + 1) * HD].astype(jnp.float32)
            sums[g] = sums[g] + factor[:, g : g + 1] * value

    def add(d, state):
        norm, sums = state
        factor = jnp.exp(sbuf[d] - top)
        sums = tuple(
            sums[g] + factor[:, g : g + 1] * pbuf[d, g].astype(jnp.float32) for g in range(KVH)
        )
        return norm + factor, sums

    norm, sums = lax.fori_loop(0, depth, add, (norm, tuple(sums)))
    for g in range(KVH):
        out_ref[g] = (sums[g] / norm[:, g : g + 1]).astype(out_ref.dtype)

    pair(0, q_y_out, q_y_out, across).wait_send()
    pair(1, q_c_out, q_c_out, sibling).wait_send()
    for copy in (part1, part1s, part2, part2s):
        copy.wait_send()

    def finish_row(z):
        for kind in (QROW, PART, STAT):
            row(kind, z).wait_send()

    each(depth, my_z, finish_row)
    own_page(KEYS).wait()
    own_page(VALUES).wait()

    def finish(peer):
        page(KEYS, peer, True).wait_recv()
        page(VALUES, peer, True).wait_recv()
        for kind in (META, KEYS, VALUES):
            page(kind, peer).wait_send()

    each(n, me, finish)


def main(n, cap, counts, q, meta, ck, cv, pk, pv, own_k, own_v):
    height = n * ROWS
    chunk = min(height, 384)
    vmem = pl.BlockSpec(memory_space=pltpu.VMEM)
    smem = pl.BlockSpec(memory_space=pltpu.SMEM)
    hbm = pl.BlockSpec(memory_space=pl.ANY)

    def parts(rows):
        return pltpu.VMEM((KVH, rows, HD), jnp.bfloat16)

    def stats(rows):
        return pltpu.VMEM((rows, LANES), jnp.float32)

    half, quarter, depth = height // 2, height // 4, n // 4
    return pl.pallas_call(
        functools.partial(main_kernel, n, cap, chunk),
        in_specs=[smem, vmem, vmem, vmem, vmem, hbm, hbm, vmem, vmem],
        out_specs=(vmem, hbm, hbm, vmem),
        out_shape=(
            jax.ShapeDtypeStruct((KVH, ROWS, HD), jnp.bfloat16),
            jax.ShapeDtypeStruct(pk.shape, pk.dtype),
            jax.ShapeDtypeStruct(pv.shape, pv.dtype),
            jax.ShapeDtypeStruct(meta.shape, meta.dtype),
        ),
        scratch_shapes=[
            parts(height), parts(height), stats(height), pltpu.VMEM((height, LANES), jnp.int32),
            parts(half), stats(half), parts(half), stats(half),
            parts(quarter), stats(quarter), parts(quarter), stats(quarter),
            pltpu.VMEM((depth, KVH, ROWS, HD), jnp.bfloat16),
            pltpu.VMEM((depth, ROWS, LANES), jnp.float32),
            pltpu.SemaphoreType.DMA((3, n)),
            pltpu.SemaphoreType.DMA((3, n)),
            pltpu.SemaphoreType.DMA((3, depth)),
            pltpu.SemaphoreType.DMA((3, depth)),
            pltpu.SemaphoreType.DMA((6,)),
            pltpu.SemaphoreType.DMA((6,)),
            pltpu.SemaphoreType.DMA((6,)),
        ],
        compiler_params=pltpu.CompilerParams(
            collective_id=0, has_side_effects=True, vmem_limit_bytes=48 << 20
        ),
        name="exchange",
    )(counts, q, meta, ck, cv, pk, pv, own_k, own_v)


def per_device(
    prefill_q, cache_k, cache_v, page_counts, page_owner, decode_q, decode_k, decode_v, context_len
):
    n = lax.axis_size("seq")
    me = lax.axis_index("seq")
    page_slots = cache_k.shape[0] // PAGE
    cap = max(2, 2 * page_slots // n)
    ck = cache_k.reshape(page_slots, PAGE, KVD)
    cv = cache_v.reshape(page_slots, PAGE, KVD)
    pk, pv, meta = pack(n, cap, page_owner[:, 0], page_counts, context_len, ck, cv)
    q = jnp.concatenate((prefill_q, decode_q[0]), axis=0)
    q = q.reshape(1 + STEPS, KVH, GROUP, HD).transpose(1, 0, 2, 3).reshape(KVH, ROWS, HD)
    out, store_k, store_v, meta = main(
        n, cap, page_counts, q, meta, cache_k, cache_v, pk, pv, decode_k[0], decode_v[0]
    )
    out = out.reshape(KVH, 1 + STEPS, GROUP, HD).transpose(1, 0, 2, 3).reshape(1 + STEPS, HQ * HD)
    return (
        out[:1],
        out[1:].reshape(1, STEPS, HQ * HD),
        store_k.reshape(-1, KVD),
        store_v.reshape(-1, KVD),
        meta[:, :cap, ID_LANE].reshape(-1),
    )


def solution(mesh):
    both = ("groups", "seq")
    in_specs = (
        P(both, None),
        P(both, None),
        P(both, None),
        P("groups"),
        P(both, None),
        P(both, None, None),
        P(both, None, None),
        P(both, None, None),
        P(both),
    )
    out_specs = (
        P(both, None),
        P(both, None, None),
        P(both, None),
        P(both, None),
        P(both),
    )
    return jax.shard_map(
        per_device, mesh=mesh, in_specs=in_specs, out_specs=out_specs, check_vma=False
    )
```

```python
import functools

import jax
import jax.numpy as jnp
from jax import lax
from jax.experimental import pallas as pl
from jax.experimental.pallas import tpu as pltpu
from jax.sharding import PartitionSpec as P

HQ = 64
KVH = 8
HD = 128
PAGE = 8
STEPS = 2
KVD = 1024
GROUP = HQ // KVH
ROWS = (1 + STEPS) * GROUP
LANES = 128
ID_LANE = 64
MASKED = -1e30
SCALE = HD ** (-0.5)
MESH = pl.DeviceIdType.MESH

META, KEYS, VALUES = range(3)
QROW, PART, STAT = range(3)


def pack_kernel(n, cap, page_slots, owner, counts, context, ck, cv, out_k, out_v, meta, table, seen):
    me = lax.axis_index("seq")

    def clear(i, _):
        seen[i] = 0
        for k in range(cap):
            table[i * cap + k] = -1
        return 0

    lax.fori_loop(0, n, clear, 0)

    def place(j, _):
        o = owner[j]
        k = seen[o]
        seen[o] = k + 1
        table[o * cap + k] = j
        return 0

    lax.fori_loop(0, counts[me], place, 0)

    tile_row = lax.broadcasted_iota(jnp.int32, (8, LANES), 0)
    lane = lax.broadcasted_iota(jnp.int32, (8, LANES), 1)

    def fill(dst, _):
        ids = jnp.full((8, LANES), -1, jnp.int32)
        for k in range(cap):
            slot = dst * cap + k
            src = table[slot]
            page = jnp.maximum(src, 0)
            there = jnp.full((PAGE, KVD), src, jnp.int32) >= 0
            out_k[slot] = jnp.where(there, ck[page], jnp.zeros((), out_k.dtype))
            out_v[slot] = jnp.where(there, cv[page], jnp.zeros((), out_v.dtype))
            ids = jnp.where(tile_row == k, jnp.where(src >= 0, me * page_slots + src, -1), ids)
        meta[dst] = jnp.where(lane < ID_LANE, context[0], ids)
        return 0

    lax.fori_loop(0, n, fill, 0)


def pack(n, cap, owner, counts, context, ck, cv):
    page_slots = ck.shape[0]
    smem = pl.BlockSpec(memory_space=pltpu.SMEM)
    vmem = pl.BlockSpec(memory_space=pltpu.VMEM)
    return pl.pallas_call(
        functools.partial(pack_kernel, n, cap, page_slots),
        in_specs=[smem, smem, smem, vmem, vmem],
        out_specs=(vmem, vmem, vmem),
        out_shape=(
            jax.ShapeDtypeStruct((n * cap, PAGE, KVD), ck.dtype),
            jax.ShapeDtypeStruct((n * cap, PAGE, KVD), cv.dtype),
            jax.ShapeDtypeStruct((n, 8, LANES), jnp.int32),
        ),
        scratch_shapes=[pltpu.SMEM((n * cap,), jnp.int32), pltpu.SMEM((n,), jnp.int32)],
        compiler_params=pltpu.CompilerParams(vmem_limit_bytes=16 << 20),
        name="pack",
    )(owner, counts, context, ck, cv)


def main_kernel(
    n, cap, chunk, counts, q_ref, meta_ref, ck_ref, cv_ref, pk_ref, pv_ref, ok_ref, ov_ref,
    out_ref, store_k, store_v, meta_out,
    qbuf, obuf, stat, limit, got1, got1s, obuf1, stat1, got2, got2s, obuf2, stat2, pbuf, sbuf,
    page_send, page_recv, row_send, row_recv, pair_send, pair_recv, local,
):
    depth = n // 4
    me = lax.axis_index("seq")
    my_z, my_y, my_c = me // 4, (me // 2) % 2, me % 2
    block = (my_c * 2 + my_y) * depth + my_z
    across = my_z * 4 + (1 - my_y) * 2 + my_c
    sibling = my_z * 4 + my_y * 2 + (1 - my_c)

    def rows_of(first, count=1):
        return pl.ds(pl.multiple_of(first * ROWS, 8), count * ROWS)

    def slots_of(d):
        return pl.ds(d * cap, cap)

    def page_ends(kind, peer, writer):
        if kind == META:
            return meta_ref.at[peer], meta_out.at[writer]
        if kind == KEYS:
            return pk_ref.at[slots_of(peer)], store_k.at[slots_of(writer)]
        return pv_ref.at[slots_of(peer)], store_v.at[slots_of(writer)]

    def page(kind, peer, arriving=False):
        src, dst = page_ends(kind, peer, peer if arriving else me)
        return pltpu.make_async_remote_copy(
            src_ref=src, dst_ref=dst, send_sem=page_send.at[kind, peer],
            recv_sem=page_recv.at[kind, peer if arriving else me],
            device_id={"seq": peer}, device_id_type=MESH,
        )

    def row_ends(kind, z, writer):
        if kind == QROW:
            return q_ref, qbuf.at[:, rows_of((my_c * 2 + my_y) * depth + writer), :]
        if kind == PART:
            return obuf2.at[:, rows_of(z), :], pbuf.at[writer]
        return stat2.at[rows_of(z), :], sbuf.at[writer]

    def row(kind, z, arriving=False):
        src, dst = row_ends(kind, z, z if arriving else my_z)
        return pltpu.make_async_remote_copy(
            src_ref=src, dst_ref=dst, send_sem=row_send.at[kind, z],
            recv_sem=row_recv.at[kind, z if arriving else my_z],
            device_id={"seq": z * 4 + my_y * 2 + my_c}, device_id_type=MESH,
        )

    def pair(number, src, dst, peer):
        return pltpu.make_async_remote_copy(
            src_ref=src, dst_ref=dst, send_sem=pair_send.at[number], recv_sem=pair_recv.at[number],
            device_id={"seq": peer}, device_id_type=MESH,
        )

    def own_page(kind):
        src, dst = page_ends(kind, me, me)
        return pltpu.make_async_copy(src, dst, local.at[kind])

    def own_row(kind):
        src, dst = row_ends(kind, my_z, my_z)
        return pltpu.make_async_copy(src, dst, local.at[3 + kind])

    def each(count, mine, body):
        def step(i, _):
            body(lax.rem(mine + i, count))
            return 0

        lax.fori_loop(1, count, step, 0)

    barrier = pltpu.get_barrier_semaphore()

    def greet(peer):
        pl.semaphore_signal(barrier, inc=1, device_id={"seq": peer}, device_id_type=MESH)

    each(n, me, greet)
    pl.semaphore_wait(barrier, n - 1)

    each(depth, my_z, lambda z: row(QROW, z).start())
    own_row(QROW).start()
    each(n, me, lambda peer: page(META, peer).start())
    for kind in (META, KEYS, VALUES):
        own_page(kind).start()

    def start_pages(peer):
        page(KEYS, peer).start()
        page(VALUES, peer).start()

    def near(i, _):
        z = lax.rem(my_z + depth // 2 + i, depth)

        @pl.when(z != my_z)
        def _():
            start_pages(z * 4 + my_y * 2 + my_c)
            start_pages(z * 4 + my_y * 2 + (1 - my_c))

        return 0

    lax.fori_loop(0, depth, near, 0)

    own_row(QROW).wait()
    each(depth, my_z, lambda z: row(QROW, z, True).wait_recv())
    q_y_out = qbuf.at[:, rows_of((my_c * 2 + my_y) * depth, depth), :]
    q_y_in = qbuf.at[:, rows_of((my_c * 2 + 1 - my_y) * depth, depth), :]
    pair(0, q_y_out, q_y_out, across).start()
    pair(0, q_y_out, q_y_in, across).wait_recv()
    q_c_out = qbuf.at[:, rows_of(my_c * 2 * depth, 2 * depth), :]
    q_c_in = qbuf.at[:, rows_of((1 - my_c) * 2 * depth, 2 * depth), :]
    pair(1, q_c_out, q_c_out, sibling).start()
    own_page(META).wait()
    each(n, me, lambda peer: page(META, peer, True).wait_recv())

    live = PAGE * counts[me]
    start = PAGE * lax.fori_loop(
        0, n, lambda i, sofar: sofar + jnp.where(i < me, counts[i], 0), jnp.int32(0)
    )
    prompt = PAGE * lax.fori_loop(0, n, lambda i, sofar: sofar + counts[i], jnp.int32(0))

    def set_limit(p, _):
        d = (p % depth) * 4 + ((p // depth) % 2) * 2 + p // (2 * depth)
        base = pl.multiple_of(p * ROWS, 8)
        context = jnp.broadcast_to(meta_out[d][:, 0:1], (8, LANES))
        reach = jnp.minimum(live, context - start)
        limit[pl.ds(base, 8), :] = jnp.full(
            (8, LANES), jnp.minimum(live, prompt - n + d + 1 - start)
        )
        for s in range(STEPS):
            limit[pl.ds(pl.multiple_of(base + 8 * (s + 1), 8), 8), :] = reach
        return 0

    lax.fori_loop(0, n, set_limit, 0)
    pair(1, q_c_out, q_c_in, sibling).wait_recv()

    lane = lax.broadcasted_iota(jnp.int32, (chunk, LANES), 1)
    keys = ck_ref.shape[0]

    def attend(c, _):
        rows = pl.ds(pl.multiple_of(c * chunk, 16), chunk)

        def head(g, stats):
            cols = pl.ds(pl.multiple_of(g * HD, HD), HD)
            scores = lax.dot_general(
                qbuf[g, rows, :], ck_ref[:, cols], (((1,), (1,)), ((), ())),
                preferred_element_type=jnp.float32,
            ) * SCALE
            place = lax.broadcasted_iota(jnp.int32, (chunk, keys), 1)
            bound = limit[rows, 0:1]
            scores = jnp.where(place < bound, scores, MASKED)
            high = jnp.max(scores, axis=1, keepdims=True)
            weights = jnp.exp(scores - high)
            total = jnp.sum(weights, axis=1, keepdims=True)
            summed = jnp.dot(
                weights.astype(jnp.bfloat16), cv_ref[:, cols], preferred_element_type=jnp.float32
            )
            obuf[g, rows, :] = (summed / total).astype(jnp.bfloat16)
            level = jnp.where(bound > 0, high + jnp.log(total), MASKED)
            return jnp.where(lane == g, level, stats)

        stat[rows, :] = lax.fori_loop(0, KVH, head, jnp.zeros((chunk, LANES), jnp.float32))
        return 0

    lax.fori_loop(0, stat.shape[0] // chunk, attend, 0)

    def merge(a, a_stat, first, b, b_stat, to, to_stat):
        step = 2 * ROWS

        def some(i, _):
            here = pl.ds(pl.multiple_of(i * step, 16), step)
            there = pl.ds(pl.multiple_of(first * ROWS + i * step, 16), step)
            one, two = a_stat[there, :], b_stat[here, :]
            high = jnp.maximum(one, two)
            one, two = jnp.exp(one - high), jnp.exp(two - high)
            both = one + two
            to_stat[here, :] = high + jnp.log(both)
            one, two = one / both, two / both
            for g in range(KVH):
                to[g, here, :] = (
                    one[:, g : g + 1] * a[g, there, :].astype(jnp.float32)
                    + two[:, g : g + 1] * b[g, here, :].astype(jnp.float32)
                ).astype(jnp.bfloat16)
            return 0

        lax.fori_loop(0, to_stat.shape[0] // step, some, 0)

    give = (1 - my_c) * 2 * depth
    part1 = pair(2, obuf.at[:, rows_of(give, 2 * depth), :], got1, sibling)
    part1s = pair(3, stat.at[rows_of(give, 2 * depth), :], got1s, sibling)
    part1s.start()
    part1.start()
    part1s.wait_recv()
    part1.wait_recv()
    merge(obuf, stat, my_c * 2 * depth, got1, got1s, obuf1, stat1)
    give = (1 - my_y) * depth
    part2 = pair(4, obuf1.at[:, rows_of(give, depth), :], got2, across)
    part2s = pair(5, stat1.at[rows_of(give, depth), :], got2s, across)
    part2s.start()
    part2.start()
    start_pages(sibling)

    own_lane = lax.broadcasted_iota(jnp.int32, (ROWS, LANES), 1)
    own_place = lax.broadcasted_iota(jnp.int32, (ROWS, LANES), 0)
    own_levels = []
    for t in range(STEPS):
        level = jnp.zeros((ROWS, LANES), jnp.float32)
        for g in range(KVH):
            key = ok_ref[t : t + 1, g * HD : (g + 1) * HD].astype(jnp.float32)
            score = jnp.sum(q_ref[g].astype(jnp.float32) * key, axis=1, keepdims=True) * SCALE
            level = jnp.where(own_lane == g, score, level)
        own_levels.append(jnp.where(own_place >= GROUP * (t + 1), level, MASKED))

    part2s.wait_recv()
    part2.wait_recv()
    merge(obuf1, stat1, my_y * depth, got2, got2s, obuf2, stat2)

    def start_rows(z):
        row(STAT, z).start()
        row(PART, z).start()

    each(depth, my_z, start_rows)
    own_row(STAT).start()
    own_row(PART).start()

    def far(i, _):
        z = lax.rem(my_z + depth // 2 + i, depth)
        start_pages(z * 4 + (1 - my_y) * 2 + my_c)
        start_pages(z * 4 + (1 - my_y) * 2 + (1 - my_c))
        return 0

    lax.fori_loop(0, depth, far, 0)

    own_row(STAT).wait()
    own_row(PART).wait()

    def wait_rows(z):
        row(STAT, z, True).wait_recv()
        row(PART, z, True).wait_recv()

    each(depth, my_z, wait_rows)

    top = functools.reduce(jnp.maximum, own_levels)
    top = lax.fori_loop(0, depth, lambda d, high: jnp.maximum(high, sbuf[d]), top)

    norm = jnp.zeros((ROWS, LANES), jnp.float32)
    sums = [jnp.zeros((ROWS, HD), jnp.float32) for _ in range(KVH)]
    for t in range(STEPS):
        factor = jnp.exp(own_levels[t] - top)
        norm = norm + factor
        for g in range(KVH):
            value = ov_ref[t : t + 1, g * HD : (g + 1) * HD].astype(jnp.float32)
            sums[g] = sums[g] + factor[:, g : g + 1] * value

    def add(d, state):
        norm, sums = state
        factor = jnp.exp(sbuf[d] - top)
        sums = tuple(
            sums[g] + factor[:, g : g + 1] * pbuf[d, g].astype(jnp.float32) for g in range(KVH)
        )
        return norm + factor, sums

    norm, sums = lax.fori_loop(0, depth, add, (norm, tuple(sums)))
    for g in range(KVH):
        out_ref[g] = (sums[g] / norm[:, g : g + 1]).astype(out_ref.dtype)

    pair(0, q_y_out, q_y_out, across).wait_send()
    pair(1, q_c_out, q_c_out, sibling).wait_send()
    for copy in (part1, part1s, part2, part2s):
        copy.wait_send()

    def finish_row(z):
        for kind in (QROW, PART, STAT):
            row(kind, z).wait_send()

    each(depth, my_z, finish_row)
    own_page(KEYS).wait()
    own_page(VALUES).wait()

    def finish(peer):
        page(KEYS, peer, True).wait_recv()
        page(VALUES, peer, True).wait_recv()
        for kind in (META, KEYS, VALUES):
            page(kind, peer).wait_send()

    each(n, me, finish)


def main(n, cap, counts, q, meta, ck, cv, pk, pv, own_k, own_v):
    height = n * ROWS
    chunk = min(height, 384)
    vmem = pl.BlockSpec(memory_space=pltpu.VMEM)
    smem = pl.BlockSpec(memory_space=pltpu.SMEM)

    def parts(rows):
        return pltpu.VMEM((KVH, rows, HD), jnp.bfloat16)

    def stats(rows):
        return pltpu.VMEM((rows, LANES), jnp.float32)

    half, quarter, depth = height // 2, height // 4, n // 4
    return pl.pallas_call(
        functools.partial(main_kernel, n, cap, chunk),
        in_specs=[smem] + [vmem] * 8,
        out_specs=(vmem, vmem, vmem, vmem),
        out_shape=(
            jax.ShapeDtypeStruct((KVH, ROWS, HD), jnp.bfloat16),
            jax.ShapeDtypeStruct(pk.shape, pk.dtype),
            jax.ShapeDtypeStruct(pv.shape, pv.dtype),
            jax.ShapeDtypeStruct(meta.shape, meta.dtype),
        ),
        scratch_shapes=[
            parts(height), parts(height), stats(height), pltpu.VMEM((height, LANES), jnp.int32),
            parts(half), stats(half), parts(half), stats(half),
            parts(quarter), stats(quarter), parts(quarter), stats(quarter),
            pltpu.VMEM((depth, KVH, ROWS, HD), jnp.bfloat16),
            pltpu.VMEM((depth, ROWS, LANES), jnp.float32),
            pltpu.SemaphoreType.DMA((3, n)),
            pltpu.SemaphoreType.DMA((3, n)),
            pltpu.SemaphoreType.DMA((3, depth)),
            pltpu.SemaphoreType.DMA((3, depth)),
            pltpu.SemaphoreType.DMA((6,)),
            pltpu.SemaphoreType.DMA((6,)),
            pltpu.SemaphoreType.DMA((6,)),
        ],
        compiler_params=pltpu.CompilerParams(
            collective_id=0, has_side_effects=True, vmem_limit_bytes=32 << 20
        ),
        name="exchange",
    )(counts, q, meta, ck, cv, pk, pv, own_k, own_v)


def write_kernel(k_in, v_in, k_out, v_out, done):
    copies = [
        pltpu.make_async_copy(k_in, k_out, done.at[0]),
        pltpu.make_async_copy(v_in, v_out, done.at[1]),
    ]
    for copy in copies:
        copy.start()
    for copy in copies:
        copy.wait()


def write(store_k, store_v):
    vmem = pl.BlockSpec(memory_space=pltpu.VMEM)
    hbm = pl.BlockSpec(memory_space=pl.ANY)
    return pl.pallas_call(
        write_kernel,
        in_specs=[vmem, vmem],
        out_specs=(hbm, hbm),
        out_shape=(
            jax.ShapeDtypeStruct(store_k.shape, store_k.dtype),
            jax.ShapeDtypeStruct(store_v.shape, store_v.dtype),
        ),
        scratch_shapes=[pltpu.SemaphoreType.DMA((2,))],
        compiler_params=pltpu.CompilerParams(vmem_limit_bytes=16 << 20),
        name="write",
    )(store_k, store_v)


def per_device(
    prefill_q, cache_k, cache_v, page_counts, page_owner, decode_q, decode_k, decode_v, context_len
):
    n = lax.axis_size("seq")
    me = lax.axis_index("seq")
    page_slots = cache_k.shape[0] // PAGE
    cap = max(2, 2 * page_slots // n)
    ck = cache_k.reshape(page_slots, PAGE, KVD)
    cv = cache_v.reshape(page_slots, PAGE, KVD)
    pk, pv, meta = pack(n, cap, page_owner[:, 0], page_counts, context_len, ck, cv)
    q = jnp.concatenate((prefill_q, decode_q[0]), axis=0)
    q = q.reshape(1 + STEPS, KVH, GROUP, HD).transpose(1, 0, 2, 3).reshape(KVH, ROWS, HD)
    out, store_k, store_v, meta = main(
        n, cap, page_counts, q, meta, cache_k, cache_v, pk, pv, decode_k[0], decode_v[0]
    )
    store_k, store_v = write(store_k, store_v)
    store_k, store_v, out, meta = lax.optimization_barrier((store_k, store_v, out, meta))
    out = out.reshape(KVH, 1 + STEPS, GROUP, HD).transpose(1, 0, 2, 3).reshape(1 + STEPS, HQ * HD)
    return (
        out[:1],
        out[1:].reshape(1, STEPS, HQ * HD),
        store_k.reshape(-1, KVD),
        store_v.reshape(-1, KVD),
        meta[:, :cap, ID_LANE].reshape(-1),
    )


def solution(mesh):
    both = ("groups", "seq")
    in_specs = (
        P(both, None),
        P(both, None),
        P(both, None),
        P("groups"),
        P(both, None),
        P(both, None, None),
        P(both, None, None),
        P(both, None, None),
        P(both),
    )
    out_specs = (
        P(both, None),
        P(both, None, None),
        P(both, None),
        P(both, None),
        P(both),
    )
    return jax.shard_map(
        per_device, mesh=mesh, in_specs=in_specs, out_specs=out_specs, check_vma=False
    )
```

```python
import functools

import jax
import jax.numpy as jnp
from jax import lax
from jax.experimental import pallas as pl
from jax.experimental.pallas import tpu as pltpu
from jax.sharding import PartitionSpec as P

HQ = 64
KVH = 8
HD = 128
PAGE = 8
STEPS = 2
KVD = 1024
GROUP = HQ // KVH
ROWS = (1 + STEPS) * GROUP
LANES = 128
ID_LANE = 64
MASKED = -1e30
SCALE = HD ** (-0.5)
MESH = pl.DeviceIdType.MESH

META, KEYS, VALUES = range(3)
QROW, PART, STAT = range(3)


def pack_kernel(
    n, cap, page_slots, owner, counts, context, ck_hbm, cv_hbm, out_k, out_v, meta,
    ck, cv, table, seen, done,
):
    me = lax.axis_index("seq")
    loads = [
        pltpu.make_async_copy(ck_hbm, ck, done.at[0]),
        pltpu.make_async_copy(cv_hbm, cv, done.at[1]),
    ]
    for load in loads:
        load.start()

    def clear(i, _):
        seen[i] = 0
        for k in range(cap):
            table[i * cap + k] = -1
        return 0

    lax.fori_loop(0, n, clear, 0)

    def place(j, _):
        o = owner[j]
        k = seen[o]
        seen[o] = k + 1
        table[o * cap + k] = j
        return 0

    lax.fori_loop(0, counts[me], place, 0)

    for load in loads:
        load.wait()

    tile_row = lax.broadcasted_iota(jnp.int32, (8, LANES), 0)
    lane = lax.broadcasted_iota(jnp.int32, (8, LANES), 1)

    def fill(dst, _):
        ids = jnp.full((8, LANES), -1, jnp.int32)
        for k in range(cap):
            slot = dst * cap + k
            src = table[slot]
            page = jnp.maximum(src, 0)
            there = jnp.full((PAGE, KVD), src, jnp.int32) >= 0
            out_k[slot] = jnp.where(there, ck[page], jnp.zeros((), out_k.dtype))
            out_v[slot] = jnp.where(there, cv[page], jnp.zeros((), out_v.dtype))
            ids = jnp.where(tile_row == k, jnp.where(src >= 0, me * page_slots + src, -1), ids)
        meta[dst] = jnp.where(lane < ID_LANE, context[0], ids)
        return 0

    lax.fori_loop(0, n, fill, 0)


def pack(n, cap, owner, counts, context, ck, cv):
    page_slots = ck.shape[0]
    smem = pl.BlockSpec(memory_space=pltpu.SMEM)
    vmem = pl.BlockSpec(memory_space=pltpu.VMEM)
    hbm = pl.BlockSpec(memory_space=pl.ANY)
    return pl.pallas_call(
        functools.partial(pack_kernel, n, cap, page_slots),
        in_specs=[smem, smem, smem, hbm, hbm],
        out_specs=(vmem, vmem, vmem),
        out_shape=(
            jax.ShapeDtypeStruct((n * cap, PAGE, KVD), ck.dtype),
            jax.ShapeDtypeStruct((n * cap, PAGE, KVD), cv.dtype),
            jax.ShapeDtypeStruct((n, 8, LANES), jnp.int32),
        ),
        scratch_shapes=[
            pltpu.VMEM(ck.shape, ck.dtype), pltpu.VMEM(cv.shape, cv.dtype),
            pltpu.SMEM((n * cap,), jnp.int32), pltpu.SMEM((n,), jnp.int32),
            pltpu.SemaphoreType.DMA((2,)),
        ],
        compiler_params=pltpu.CompilerParams(vmem_limit_bytes=16 << 20),
        name="pack",
    )(owner, counts, context, ck, cv)


def main_kernel(
    n, cap, chunk, counts, q_ref, meta_ref, ck_ref, cv_ref, pk_ref, pv_ref, ok_ref, ov_ref,
    out_ref, store_k, store_v, meta_out,
    qbuf, obuf, stat, limit, got1, got1s, obuf1, stat1, got2, got2s, obuf2, stat2, pbuf, sbuf,
    page_send, page_recv, row_send, row_recv, pair_send, pair_recv, local,
):
    depth = n // 4
    me = lax.axis_index("seq")
    my_z, my_y, my_c = me // 4, (me // 2) % 2, me % 2
    block = (my_c * 2 + my_y) * depth + my_z
    across = my_z * 4 + (1 - my_y) * 2 + my_c
    sibling = my_z * 4 + my_y * 2 + (1 - my_c)

    def rows_of(first, count=1):
        return pl.ds(pl.multiple_of(first * ROWS, 8), count * ROWS)

    def slots_of(d):
        return pl.ds(d * cap, cap)

    def page_ends(kind, peer, writer):
        if kind == META:
            return meta_ref.at[peer], meta_out.at[writer]
        if kind == KEYS:
            return pk_ref.at[slots_of(peer)], store_k.at[slots_of(writer)]
        return pv_ref.at[slots_of(peer)], store_v.at[slots_of(writer)]

    def page(kind, peer, arriving=False):
        src, dst = page_ends(kind, peer, peer if arriving else me)
        return pltpu.make_async_remote_copy(
            src_ref=src, dst_ref=dst, send_sem=page_send.at[kind, peer],
            recv_sem=page_recv.at[kind, peer if arriving else me],
            device_id={"seq": peer}, device_id_type=MESH,
        )

    def row_ends(kind, z, writer):
        if kind == QROW:
            return q_ref, qbuf.at[:, rows_of((my_c * 2 + my_y) * depth + writer), :]
        if kind == PART:
            return obuf2.at[:, rows_of(z), :], pbuf.at[writer]
        return stat2.at[rows_of(z), :], sbuf.at[writer]

    def row(kind, z, arriving=False):
        src, dst = row_ends(kind, z, z if arriving else my_z)
        return pltpu.make_async_remote_copy(
            src_ref=src, dst_ref=dst, send_sem=row_send.at[kind, z],
            recv_sem=row_recv.at[kind, z if arriving else my_z],
            device_id={"seq": z * 4 + my_y * 2 + my_c}, device_id_type=MESH,
        )

    def pair(number, src, dst, peer):
        return pltpu.make_async_remote_copy(
            src_ref=src, dst_ref=dst, send_sem=pair_send.at[number], recv_sem=pair_recv.at[number],
            device_id={"seq": peer}, device_id_type=MESH,
        )

    def own_page(kind):
        src, dst = page_ends(kind, me, me)
        return pltpu.make_async_copy(src, dst, local.at[kind])

    def own_row(kind):
        src, dst = row_ends(kind, my_z, my_z)
        return pltpu.make_async_copy(src, dst, local.at[3 + kind])

    def each(count, mine, body):
        def step(i, _):
            body(lax.rem(mine + i, count))
            return 0

        lax.fori_loop(1, count, step, 0)

    barrier = pltpu.get_barrier_semaphore()

    def greet(peer):
        pl.semaphore_signal(barrier, inc=1, device_id={"seq": peer}, device_id_type=MESH)

    each(n, me, greet)
    pl.semaphore_wait(barrier, n - 1)

    each(depth, my_z, lambda z: row(QROW, z).start())
    own_row(QROW).start()
    each(n, me, lambda peer: page(META, peer).start())
    for kind in (META, KEYS, VALUES):
        own_page(kind).start()

    def start_pages(peer):
        page(KEYS, peer).start()
        page(VALUES, peer).start()

    def near(i, _):
        z = lax.rem(my_z + depth // 2 + i, depth)

        @pl.when(z != my_z)
        def _():
            start_pages(z * 4 + my_y * 2 + my_c)
            start_pages(z * 4 + my_y * 2 + (1 - my_c))

        return 0

    lax.fori_loop(0, depth, near, 0)

    own_row(QROW).wait()
    each(depth, my_z, lambda z: row(QROW, z, True).wait_recv())
    q_y_out = qbuf.at[:, rows_of((my_c * 2 + my_y) * depth, depth), :]
    q_y_in = qbuf.at[:, rows_of((my_c * 2 + 1 - my_y) * depth, depth), :]
    pair(0, q_y_out, q_y_out, across).start()
    pair(0, q_y_out, q_y_in, across).wait_recv()
    q_c_out = qbuf.at[:, rows_of(my_c * 2 * depth, 2 * depth), :]
    q_c_in = qbuf.at[:, rows_of((1 - my_c) * 2 * depth, 2 * depth), :]
    pair(1, q_c_out, q_c_out, sibling).start()
    own_page(META).wait()
    each(n, me, lambda peer: page(META, peer, True).wait_recv())

    live = PAGE * counts[me]
    start = PAGE * lax.fori_loop(
        0, n, lambda i, sofar: sofar + jnp.where(i < me, counts[i], 0), jnp.int32(0)
    )
    prompt = PAGE * lax.fori_loop(0, n, lambda i, sofar: sofar + counts[i], jnp.int32(0))

    def set_limit(p, _):
        d = (p % depth) * 4 + ((p // depth) % 2) * 2 + p // (2 * depth)
        base = pl.multiple_of(p * ROWS, 8)
        context = jnp.broadcast_to(meta_out[d][:, 0:1], (8, LANES))
        reach = jnp.minimum(live, context - start)
        limit[pl.ds(base, 8), :] = jnp.full(
            (8, LANES), jnp.minimum(live, prompt - n + d + 1 - start)
        )
        for s in range(STEPS):
            limit[pl.ds(pl.multiple_of(base + 8 * (s + 1), 8), 8), :] = reach
        return 0

    lax.fori_loop(0, n, set_limit, 0)
    pair(1, q_c_out, q_c_in, sibling).wait_recv()

    def far(i, _):
        z = lax.rem(my_z + depth // 2 + i, depth)
        start_pages(z * 4 + (1 - my_y) * 2 + my_c)
        start_pages(z * 4 + (1 - my_y) * 2 + (1 - my_c))
        return 0

    far(0, 0)

    lane = lax.broadcasted_iota(jnp.int32, (chunk, LANES), 1)
    keys = ck_ref.shape[0]

    def attend(c, _):
        rows = pl.ds(pl.multiple_of(c * chunk, 16), chunk)

        def head(g, stats):
            cols = pl.ds(pl.multiple_of(g * HD, HD), HD)
            scores = lax.dot_general(
                qbuf[g, rows, :], ck_ref[:, cols], (((1,), (1,)), ((), ())),
                preferred_element_type=jnp.float32,
            ) * SCALE
            place = lax.broadcasted_iota(jnp.int32, (chunk, keys), 1)
            bound = limit[rows, 0:1]
            scores = jnp.where(place < bound, scores, MASKED)
            high = jnp.max(scores, axis=1, keepdims=True)
            weights = jnp.exp(scores - high)
            total = jnp.sum(weights, axis=1, keepdims=True)
            summed = jnp.dot(
                weights.astype(jnp.bfloat16), cv_ref[:, cols], preferred_element_type=jnp.float32
            )
            obuf[g, rows, :] = (summed / total).astype(jnp.bfloat16)
            level = jnp.where(bound > 0, high + jnp.log(total), MASKED)
            return jnp.where(lane == g, level, stats)

        stat[rows, :] = lax.fori_loop(0, KVH, head, jnp.zeros((chunk, LANES), jnp.float32))
        return 0

    lax.fori_loop(0, stat.shape[0] // chunk, attend, 0)

    def merge(a, a_stat, first, b, b_stat, to, to_stat):
        step = 2 * ROWS

        def some(i, _):
            here = pl.ds(pl.multiple_of(i * step, 16), step)
            there = pl.ds(pl.multiple_of(first * ROWS + i * step, 16), step)
            one, two = a_stat[there, :], b_stat[here, :]
            high = jnp.maximum(one, two)
            one, two = jnp.exp(one - high), jnp.exp(two - high)
            both = one + two
            to_stat[here, :] = high + jnp.log(both)
            one, two = one / both, two / both
            for g in range(KVH):
                to[g, here, :] = (
                    one[:, g : g + 1] * a[g, there, :].astype(jnp.float32)
                    + two[:, g : g + 1] * b[g, here, :].astype(jnp.float32)
                ).astype(jnp.bfloat16)
            return 0

        lax.fori_loop(0, to_stat.shape[0] // step, some, 0)

    give = (1 - my_c) * 2 * depth
    part1 = pair(2, obuf.at[:, rows_of(give, 2 * depth), :], got1, sibling)
    part1s = pair(3, stat.at[rows_of(give, 2 * depth), :], got1s, sibling)
    part1s.start()
    part1.start()
    part1s.wait_recv()
    part1.wait_recv()
    merge(obuf, stat, my_c * 2 * depth, got1, got1s, obuf1, stat1)
    give = (1 - my_y) * depth
    part2 = pair(4, obuf1.at[:, rows_of(give, depth), :], got2, across)
    part2s = pair(5, stat1.at[rows_of(give, depth), :], got2s, across)
    part2s.start()
    part2.start()
    start_pages(sibling)

    own_lane = lax.broadcasted_iota(jnp.int32, (ROWS, LANES), 1)
    own_place = lax.broadcasted_iota(jnp.int32, (ROWS, LANES), 0)
    own_levels = []
    for t in range(STEPS):
        level = jnp.zeros((ROWS, LANES), jnp.float32)
        for g in range(KVH):
            key = ok_ref[t : t + 1, g * HD : (g + 1) * HD].astype(jnp.float32)
            score = jnp.sum(q_ref[g].astype(jnp.float32) * key, axis=1, keepdims=True) * SCALE
            level = jnp.where(own_lane == g, score, level)
        own_levels.append(jnp.where(own_place >= GROUP * (t + 1), level, MASKED))

    part2s.wait_recv()
    part2.wait_recv()
    merge(obuf1, stat1, my_y * depth, got2, got2s, obuf2, stat2)

    def start_rows(z):
        row(STAT, z).start()
        row(PART, z).start()

    each(depth, my_z, start_rows)
    own_row(STAT).start()
    own_row(PART).start()

    lax.fori_loop(1, depth, far, 0)

    own_row(STAT).wait()
    own_row(PART).wait()

    def wait_rows(z):
        row(STAT, z, True).wait_recv()
        row(PART, z, True).wait_recv()

    each(depth, my_z, wait_rows)

    top = functools.reduce(jnp.maximum, own_levels)
    top = lax.fori_loop(0, depth, lambda d, high: jnp.maximum(high, sbuf[d]), top)

    norm = jnp.zeros((ROWS, LANES), jnp.float32)
    sums = [jnp.zeros((ROWS, HD), jnp.float32) for _ in range(KVH)]
    for t in range(STEPS):
        factor = jnp.exp(own_levels[t] - top)
        norm = norm + factor
        for g in range(KVH):
            value = ov_ref[t : t + 1, g * HD : (g + 1) * HD].astype(jnp.float32)
            sums[g] = sums[g] + factor[:, g : g + 1] * value

    def add(d, state):
        norm, sums = state
        factor = jnp.exp(sbuf[d] - top)
        sums = tuple(
            sums[g] + factor[:, g : g + 1] * pbuf[d, g].astype(jnp.float32) for g in range(KVH)
        )
        return norm + factor, sums

    norm, sums = lax.fori_loop(0, depth, add, (norm, tuple(sums)))
    for g in range(KVH):
        out_ref[g] = (sums[g] / norm[:, g : g + 1]).astype(out_ref.dtype)

    pair(0, q_y_out, q_y_out, across).wait_send()
    pair(1, q_c_out, q_c_out, sibling).wait_send()
    for copy in (part1, part1s, part2, part2s):
        copy.wait_send()

    def finish_row(z):
        for kind in (QROW, PART, STAT):
            row(kind, z).wait_send()

    each(depth, my_z, finish_row)
    own_page(KEYS).wait()
    own_page(VALUES).wait()

    def finish(peer):
        page(KEYS, peer, True).wait_recv()
        page(VALUES, peer, True).wait_recv()
        for kind in (META, KEYS, VALUES):
            page(kind, peer).wait_send()

    each(n, me, finish)


def main(n, cap, counts, q, meta, ck, cv, pk, pv, own_k, own_v):
    height = n * ROWS
    chunk = min(height, 384)
    vmem = pl.BlockSpec(memory_space=pltpu.VMEM)
    smem = pl.BlockSpec(memory_space=pltpu.SMEM)

    def parts(rows):
        return pltpu.VMEM((KVH, rows, HD), jnp.bfloat16)

    def stats(rows):
        return pltpu.VMEM((rows, LANES), jnp.float32)

    half, quarter, depth = height // 2, height // 4, n // 4
    return pl.pallas_call(
        functools.partial(main_kernel, n, cap, chunk),
        in_specs=[smem] + [vmem] * 8,
        out_specs=(vmem, vmem, vmem, vmem),
        out_shape=(
            jax.ShapeDtypeStruct((KVH, ROWS, HD), jnp.bfloat16),
            jax.ShapeDtypeStruct(pk.shape, pk.dtype),
            jax.ShapeDtypeStruct(pv.shape, pv.dtype),
            jax.ShapeDtypeStruct(meta.shape, meta.dtype),
        ),
        scratch_shapes=[
            parts(height), parts(height), stats(height), pltpu.VMEM((height, LANES), jnp.int32),
            parts(half), stats(half), parts(half), stats(half),
            parts(quarter), stats(quarter), parts(quarter), stats(quarter),
            pltpu.VMEM((depth, KVH, ROWS, HD), jnp.bfloat16),
            pltpu.VMEM((depth, ROWS, LANES), jnp.float32),
            pltpu.SemaphoreType.DMA((3, n)),
            pltpu.SemaphoreType.DMA((3, n)),
            pltpu.SemaphoreType.DMA((3, depth)),
            pltpu.SemaphoreType.DMA((3, depth)),
            pltpu.SemaphoreType.DMA((6,)),
            pltpu.SemaphoreType.DMA((6,)),
            pltpu.SemaphoreType.DMA((6,)),
        ],
        compiler_params=pltpu.CompilerParams(
            collective_id=0, has_side_effects=True, vmem_limit_bytes=32 << 20
        ),
        name="exchange",
    )(counts, q, meta, ck, cv, pk, pv, own_k, own_v)


def write_kernel(k_in, v_in, k_out, v_out, done):
    copies = [
        pltpu.make_async_copy(k_in, k_out, done.at[0]),
        pltpu.make_async_copy(v_in, v_out, done.at[1]),
    ]
    for copy in copies:
        copy.start()
    for copy in copies:
        copy.wait()


def write(store_k, store_v):
    vmem = pl.BlockSpec(memory_space=pltpu.VMEM)
    hbm = pl.BlockSpec(memory_space=pl.ANY)
    return pl.pallas_call(
        write_kernel,
        in_specs=[vmem, vmem],
        out_specs=(hbm, hbm),
        out_shape=(
            jax.ShapeDtypeStruct(store_k.shape, store_k.dtype),
            jax.ShapeDtypeStruct(store_v.shape, store_v.dtype),
        ),
        scratch_shapes=[pltpu.SemaphoreType.DMA((2,))],
        compiler_params=pltpu.CompilerParams(vmem_limit_bytes=16 << 20),
        name="write",
    )(store_k, store_v)


def per_device(
    prefill_q, cache_k, cache_v, page_counts, page_owner, decode_q, decode_k, decode_v, context_len
):
    n = lax.axis_size("seq")
    me = lax.axis_index("seq")
    page_slots = cache_k.shape[0] // PAGE
    cap = max(2, 2 * page_slots // n)
    ck = cache_k.reshape(page_slots, PAGE, KVD)
    cv = cache_v.reshape(page_slots, PAGE, KVD)
    pk, pv, meta = pack(n, cap, page_owner[:, 0], page_counts, context_len, ck, cv)
    q = jnp.concatenate((prefill_q, decode_q[0]), axis=0)
    q = q.reshape(1 + STEPS, KVH, GROUP, HD).transpose(1, 0, 2, 3).reshape(KVH, ROWS, HD)
    out, store_k, store_v, meta = main(
        n, cap, page_counts, q, meta, cache_k, cache_v, pk, pv, decode_k[0], decode_v[0]
    )
    store_k, store_v = write(store_k, store_v)
    store_k, store_v, out, meta = lax.optimization_barrier((store_k, store_v, out, meta))
    out = out.reshape(KVH, 1 + STEPS, GROUP, HD).transpose(1, 0, 2, 3).reshape(1 + STEPS, HQ * HD)
    return (
        out[:1],
        out[1:].reshape(1, STEPS, HQ * HD),
        store_k.reshape(-1, KVD),
        store_v.reshape(-1, KVD),
        meta[:, :cap, ID_LANE].reshape(-1),
    )


def solution(mesh):
    both = ("groups", "seq")
    in_specs = (
        P(both, None),
        P(both, None),
        P(both, None),
        P("groups"),
        P(both, None),
        P(both, None, None),
        P(both, None, None),
        P(both, None, None),
        P(both),
    )
    out_specs = (
        P(both, None),
        P(both, None, None),
        P(both, None),
        P(both, None),
        P(both),
    )
    return jax.shard_map(
        per_device, mesh=mesh, in_specs=in_specs, out_specs=out_specs, check_vma=False
    )
```

```python
import functools

import jax
import jax.numpy as jnp
from jax import lax
from jax.experimental import pallas as pl
from jax.experimental.pallas import tpu as pltpu
from jax.sharding import PartitionSpec as P

HQ = 64
KVH = 8
HD = 128
PAGE = 8
STEPS = 2
KVD = 1024
GROUP = HQ // KVH
ROWS = (1 + STEPS) * GROUP
LANES = 128
ID_LANE = 64
MASKED = -1e30
SCALE = HD ** (-0.5)
MESH = pl.DeviceIdType.MESH

META, KEYS, VALUES = range(3)
QROW, PART, STAT = range(3)


def pack_kernel(
    n, cap, page_slots, owner, counts, context, ck_hbm, cv_hbm, out_k, out_v, meta,
    ck, cv, table, seen, done,
):
    me = lax.axis_index("seq")
    loads = [
        pltpu.make_async_copy(ck_hbm, ck, done.at[0]),
        pltpu.make_async_copy(cv_hbm, cv, done.at[1]),
    ]
    for load in loads:
        load.start()

    def clear(i, _):
        seen[i] = 0
        for k in range(cap):
            table[i * cap + k] = -1
        return 0

    lax.fori_loop(0, n, clear, 0)

    def place(j, _):
        o = owner[j]
        k = seen[o]
        seen[o] = k + 1
        table[o * cap + k] = j
        return 0

    lax.fori_loop(0, counts[me], place, 0)

    for load in loads:
        load.wait()

    tile_row = lax.broadcasted_iota(jnp.int32, (8, LANES), 0)
    lane = lax.broadcasted_iota(jnp.int32, (8, LANES), 1)

    def fill(dst, _):
        ids = jnp.full((8, LANES), -1, jnp.int32)
        for k in range(cap):
            slot = dst * cap + k
            src = table[slot]
            page = jnp.maximum(src, 0)
            there = jnp.full((PAGE, KVD), src, jnp.int32) >= 0
            out_k[slot] = jnp.where(there, ck[page], jnp.zeros((), out_k.dtype))
            out_v[slot] = jnp.where(there, cv[page], jnp.zeros((), out_v.dtype))
            ids = jnp.where(tile_row == k, jnp.where(src >= 0, me * page_slots + src, -1), ids)
        meta[dst] = jnp.where(lane < ID_LANE, context[0], ids)
        return 0

    lax.fori_loop(0, n, fill, 0)


def pack(n, cap, owner, counts, context, ck, cv):
    page_slots = ck.shape[0]
    smem = pl.BlockSpec(memory_space=pltpu.SMEM)
    vmem = pl.BlockSpec(memory_space=pltpu.VMEM)
    hbm = pl.BlockSpec(memory_space=pl.ANY)
    return pl.pallas_call(
        functools.partial(pack_kernel, n, cap, page_slots),
        in_specs=[smem, smem, smem, hbm, hbm],
        out_specs=(vmem, vmem, vmem),
        out_shape=(
            jax.ShapeDtypeStruct((n * cap, PAGE, KVD), ck.dtype),
            jax.ShapeDtypeStruct((n * cap, PAGE, KVD), cv.dtype),
            jax.ShapeDtypeStruct((n, 8, LANES), jnp.int32),
        ),
        scratch_shapes=[
            pltpu.VMEM(ck.shape, ck.dtype), pltpu.VMEM(cv.shape, cv.dtype),
            pltpu.SMEM((n * cap,), jnp.int32), pltpu.SMEM((n,), jnp.int32),
            pltpu.SemaphoreType.DMA((2,)),
        ],
        compiler_params=pltpu.CompilerParams(vmem_limit_bytes=16 << 20),
        name="pack",
    )(owner, counts, context, ck, cv)


def main_kernel(
    n, cap, chunk, counts, q_ref, meta_ref, ck_ref, cv_ref, pk_ref, pv_ref, ok_ref, ov_ref,
    out_ref, store_k, store_v, meta_out,
    qbuf, obuf, stat, limit, got1, got1s, obuf1, stat1, got2, got2s, obuf2, stat2, pbuf, sbuf,
    page_send, page_recv, row_send, row_recv, pair_send, pair_recv, local,
):
    depth = n // 4
    me = lax.axis_index("seq")
    my_z, my_y, my_c = me // 4, (me // 2) % 2, me % 2
    block = (my_c * 2 + my_y) * depth + my_z
    across = my_z * 4 + (1 - my_y) * 2 + my_c
    sibling = my_z * 4 + my_y * 2 + (1 - my_c)

    def rows_of(first, count=1):
        return pl.ds(pl.multiple_of(first * ROWS, 8), count * ROWS)

    def slots_of(d):
        return pl.ds(d * cap, cap)

    def page_ends(kind, peer, writer):
        if kind == META:
            return meta_ref.at[peer], meta_out.at[writer]
        if kind == KEYS:
            return pk_ref.at[slots_of(peer)], store_k.at[slots_of(writer)]
        return pv_ref.at[slots_of(peer)], store_v.at[slots_of(writer)]

    def page(kind, peer, arriving=False):
        src, dst = page_ends(kind, peer, peer if arriving else me)
        return pltpu.make_async_remote_copy(
            src_ref=src, dst_ref=dst, send_sem=page_send.at[kind, peer],
            recv_sem=page_recv.at[kind, peer if arriving else me],
            device_id={"seq": peer}, device_id_type=MESH,
        )

    def row_ends(kind, z, writer):
        if kind == QROW:
            return q_ref, qbuf.at[:, rows_of((my_c * 2 + my_y) * depth + writer), :]
        if kind == PART:
            return obuf2.at[:, rows_of(z), :], pbuf.at[writer]
        return stat2.at[rows_of(z), :], sbuf.at[writer]

    def row(kind, z, arriving=False):
        src, dst = row_ends(kind, z, z if arriving else my_z)
        return pltpu.make_async_remote_copy(
            src_ref=src, dst_ref=dst, send_sem=row_send.at[kind, z],
            recv_sem=row_recv.at[kind, z if arriving else my_z],
            device_id={"seq": z * 4 + my_y * 2 + my_c}, device_id_type=MESH,
        )

    def pair(number, src, dst, peer):
        return pltpu.make_async_remote_copy(
            src_ref=src, dst_ref=dst, send_sem=pair_send.at[number], recv_sem=pair_recv.at[number],
            device_id={"seq": peer}, device_id_type=MESH,
        )

    def own_page(kind):
        src, dst = page_ends(kind, me, me)
        return pltpu.make_async_copy(src, dst, local.at[kind])

    def own_row(kind):
        src, dst = row_ends(kind, my_z, my_z)
        return pltpu.make_async_copy(src, dst, local.at[3 + kind])

    def each(count, mine, body):
        def step(i, _):
            body(lax.rem(mine + i, count))
            return 0

        lax.fori_loop(1, count, step, 0)

    barrier = pltpu.get_barrier_semaphore()

    def greet(peer):
        pl.semaphore_signal(barrier, inc=1, device_id={"seq": peer}, device_id_type=MESH)

    each(n, me, greet)
    pl.semaphore_wait(barrier, n - 1)

    each(depth, my_z, lambda z: row(QROW, z).start())
    own_row(QROW).start()
    each(n, me, lambda peer: page(META, peer).start())
    for kind in (META, KEYS, VALUES):
        own_page(kind).start()

    def start_pages(peer):
        page(KEYS, peer).start()
        page(VALUES, peer).start()

    def near(i, _):
        z = lax.rem(my_z + depth // 2 + i, depth)

        @pl.when(z != my_z)
        def _():
            start_pages(z * 4 + my_y * 2 + my_c)
            start_pages(z * 4 + my_y * 2 + (1 - my_c))

        return 0

    lax.fori_loop(0, depth, near, 0)

    own_row(QROW).wait()
    each(depth, my_z, lambda z: row(QROW, z, True).wait_recv())
    q_y_out = qbuf.at[:, rows_of((my_c * 2 + my_y) * depth, depth), :]
    q_y_in = qbuf.at[:, rows_of((my_c * 2 + 1 - my_y) * depth, depth), :]
    pair(0, q_y_out, q_y_out, across).start()
    pair(0, q_y_out, q_y_in, across).wait_recv()
    q_c_out = qbuf.at[:, rows_of(my_c * 2 * depth, 2 * depth), :]
    q_c_in = qbuf.at[:, rows_of((1 - my_c) * 2 * depth, 2 * depth), :]
    pair(1, q_c_out, q_c_out, sibling).start()
    own_page(META).wait()
    each(n, me, lambda peer: page(META, peer, True).wait_recv())

    live = PAGE * counts[me]
    start = PAGE * lax.fori_loop(
        0, n, lambda i, sofar: sofar + jnp.where(i < me, counts[i], 0), jnp.int32(0)
    )
    prompt = PAGE * lax.fori_loop(0, n, lambda i, sofar: sofar + counts[i], jnp.int32(0))

    def set_limit(p, _):
        d = (p % depth) * 4 + ((p // depth) % 2) * 2 + p // (2 * depth)
        base = pl.multiple_of(p * ROWS, 8)
        context = jnp.broadcast_to(meta_out[d][:, 0:1], (8, LANES))
        reach = jnp.minimum(live, context - start)
        limit[pl.ds(base, 8), :] = jnp.full(
            (8, LANES), jnp.minimum(live, prompt - n + d + 1 - start)
        )
        for s in range(STEPS):
            limit[pl.ds(pl.multiple_of(base + 8 * (s + 1), 8), 8), :] = reach
        return 0

    lax.fori_loop(0, n, set_limit, 0)
    pair(1, q_c_out, q_c_in, sibling).wait_recv()

    def far(i, _):
        z = lax.rem(my_z + depth // 2 + i, depth)
        start_pages(z * 4 + (1 - my_y) * 2 + my_c)
        start_pages(z * 4 + (1 - my_y) * 2 + (1 - my_c))
        return 0

    far(0, 0)
    far(1, 0)

    lane = lax.broadcasted_iota(jnp.int32, (chunk, LANES), 1)
    keys = ck_ref.shape[0]

    def attend(c, _):
        rows = pl.ds(pl.multiple_of(c * chunk, 16), chunk)

        def head(g, stats):
            cols = pl.ds(pl.multiple_of(g * HD, HD), HD)
            scores = lax.dot_general(
                qbuf[g, rows, :], ck_ref[:, cols], (((1,), (1,)), ((), ())),
                preferred_element_type=jnp.float32,
            ) * SCALE
            place = lax.broadcasted_iota(jnp.int32, (chunk, keys), 1)
            bound = limit[rows, 0:1]
            scores = jnp.where(place < bound, scores, MASKED)
            high = jnp.max(scores, axis=1, keepdims=True)
            weights = jnp.exp(scores - high)
            total = jnp.sum(weights, axis=1, keepdims=True)
            summed = jnp.dot(
                weights.astype(jnp.bfloat16), cv_ref[:, cols], preferred_element_type=jnp.float32
            )
            obuf[g, rows, :] = (summed / total).astype(jnp.bfloat16)
            level = jnp.where(bound > 0, high + jnp.log(total), MASKED)
            return jnp.where(lane == g, level, stats)

        stat[rows, :] = lax.fori_loop(0, KVH, head, jnp.zeros((chunk, LANES), jnp.float32))
        return 0

    lax.fori_loop(0, stat.shape[0] // chunk, attend, 0)

    def merge(a, a_stat, first, b, b_stat, to, to_stat):
        step = 2 * ROWS

        def some(i, _):
            here = pl.ds(pl.multiple_of(i * step, 16), step)
            there = pl.ds(pl.multiple_of(first * ROWS + i * step, 16), step)
            one, two = a_stat[there, :], b_stat[here, :]
            high = jnp.maximum(one, two)
            one, two = jnp.exp(one - high), jnp.exp(two - high)
            both = one + two
            to_stat[here, :] = high + jnp.log(both)
            one, two = one / both, two / both
            for g in range(KVH):
                to[g, here, :] = (
                    one[:, g : g + 1] * a[g, there, :].astype(jnp.float32)
                    + two[:, g : g + 1] * b[g, here, :].astype(jnp.float32)
                ).astype(jnp.bfloat16)
            return 0

        lax.fori_loop(0, to_stat.shape[0] // step, some, 0)

    give = (1 - my_c) * 2 * depth
    part1 = pair(2, obuf.at[:, rows_of(give, 2 * depth), :], got1, sibling)
    part1s = pair(3, stat.at[rows_of(give, 2 * depth), :], got1s, sibling)
    part1s.start()
    part1.start()
    part1s.wait_recv()
    part1.wait_recv()
    merge(obuf, stat, my_c * 2 * depth, got1, got1s, obuf1, stat1)
    give = (1 - my_y) * depth
    part2 = pair(4, obuf1.at[:, rows_of(give, depth), :], got2, across)
    part2s = pair(5, stat1.at[rows_of(give, depth), :], got2s, across)
    part2s.start()
    part2.start()
    start_pages(sibling)

    own_lane = lax.broadcasted_iota(jnp.int32, (ROWS, LANES), 1)
    own_place = lax.broadcasted_iota(jnp.int32, (ROWS, LANES), 0)
    own_levels = []
    for t in range(STEPS):
        level = jnp.zeros((ROWS, LANES), jnp.float32)
        for g in range(KVH):
            key = ok_ref[t : t + 1, g * HD : (g + 1) * HD].astype(jnp.float32)
            score = jnp.sum(q_ref[g].astype(jnp.float32) * key, axis=1, keepdims=True) * SCALE
            level = jnp.where(own_lane == g, score, level)
        own_levels.append(jnp.where(own_place >= GROUP * (t + 1), level, MASKED))

    part2s.wait_recv()
    part2.wait_recv()
    merge(obuf1, stat1, my_y * depth, got2, got2s, obuf2, stat2)

    def start_rows(z):
        row(STAT, z).start()
        row(PART, z).start()

    each(depth, my_z, start_rows)
    own_row(STAT).start()
    own_row(PART).start()

    lax.fori_loop(2, depth, far, 0)

    own_row(STAT).wait()
    own_row(PART).wait()

    def wait_rows(z):
        row(STAT, z, True).wait_recv()
        row(PART, z, True).wait_recv()

    each(depth, my_z, wait_rows)

    top = functools.reduce(jnp.maximum, own_levels)
    top = lax.fori_loop(0, depth, lambda d, high: jnp.maximum(high, sbuf[d]), top)

    norm = jnp.zeros((ROWS, LANES), jnp.float32)
    sums = [jnp.zeros((ROWS, HD), jnp.float32) for _ in range(KVH)]
    for t in range(STEPS):
        factor = jnp.exp(own_levels[t] - top)
        norm = norm + factor
        for g in range(KVH):
            value = ov_ref[t : t + 1, g * HD : (g + 1) * HD].astype(jnp.float32)
            sums[g] = sums[g] + factor[:, g : g + 1] * value

    def add(d, state):
        norm, sums = state
        factor = jnp.exp(sbuf[d] - top)
        sums = tuple(
            sums[g] + factor[:, g : g + 1] * pbuf[d, g].astype(jnp.float32) for g in range(KVH)
        )
        return norm + factor, sums

    norm, sums = lax.fori_loop(0, depth, add, (norm, tuple(sums)))
    for g in range(KVH):
        out_ref[g] = (sums[g] / norm[:, g : g + 1]).astype(out_ref.dtype)

    pair(0, q_y_out, q_y_out, across).wait_send()
    pair(1, q_c_out, q_c_out, sibling).wait_send()
    for copy in (part1, part1s, part2, part2s):
        copy.wait_send()

    def finish_row(z):
        for kind in (QROW, PART, STAT):
            row(kind, z).wait_send()

    each(depth, my_z, finish_row)
    own_page(KEYS).wait()
    own_page(VALUES).wait()

    def finish(peer):
        page(KEYS, peer, True).wait_recv()
        page(VALUES, peer, True).wait_recv()
        for kind in (META, KEYS, VALUES):
            page(kind, peer).wait_send()

    each(n, me, finish)


def main(n, cap, counts, q, meta, ck, cv, pk, pv, own_k, own_v):
    height = n * ROWS
    chunk = min(height, 384)
    vmem = pl.BlockSpec(memory_space=pltpu.VMEM)
    smem = pl.BlockSpec(memory_space=pltpu.SMEM)

    def parts(rows):
        return pltpu.VMEM((KVH, rows, HD), jnp.bfloat16)

    def stats(rows):
        return pltpu.VMEM((rows, LANES), jnp.float32)

    half, quarter, depth = height // 2, height // 4, n // 4
    return pl.pallas_call(
        functools.partial(main_kernel, n, cap, chunk),
        in_specs=[smem] + [vmem] * 8,
        out_specs=(vmem, vmem, vmem, vmem),
        out_shape=(
            jax.ShapeDtypeStruct((KVH, ROWS, HD), jnp.bfloat16),
            jax.ShapeDtypeStruct(pk.shape, pk.dtype),
            jax.ShapeDtypeStruct(pv.shape, pv.dtype),
            jax.ShapeDtypeStruct(meta.shape, meta.dtype),
        ),
        scratch_shapes=[
            parts(height), parts(height), stats(height), pltpu.VMEM((height, LANES), jnp.int32),
            parts(half), stats(half), parts(half), stats(half),
            parts(quarter), stats(quarter), parts(quarter), stats(quarter),
            pltpu.VMEM((depth, KVH, ROWS, HD), jnp.bfloat16),
            pltpu.VMEM((depth, ROWS, LANES), jnp.float32),
            pltpu.SemaphoreType.DMA((3, n)),
            pltpu.SemaphoreType.DMA((3, n)),
            pltpu.SemaphoreType.DMA((3, depth)),
            pltpu.SemaphoreType.DMA((3, depth)),
            pltpu.SemaphoreType.DMA((6,)),
            pltpu.SemaphoreType.DMA((6,)),
            pltpu.SemaphoreType.DMA((6,)),
        ],
        compiler_params=pltpu.CompilerParams(
            collective_id=0, has_side_effects=True, vmem_limit_bytes=32 << 20
        ),
        name="exchange",
    )(counts, q, meta, ck, cv, pk, pv, own_k, own_v)


def write_kernel(k_in, v_in, k_out, v_out, done):
    copies = [
        pltpu.make_async_copy(k_in, k_out, done.at[0]),
        pltpu.make_async_copy(v_in, v_out, done.at[1]),
    ]
    for copy in copies:
        copy.start()
    for copy in copies:
        copy.wait()


def write(store_k, store_v):
    vmem = pl.BlockSpec(memory_space=pltpu.VMEM)
    hbm = pl.BlockSpec(memory_space=pl.ANY)
    return pl.pallas_call(
        write_kernel,
        in_specs=[vmem, vmem],
        out_specs=(hbm, hbm),
        out_shape=(
            jax.ShapeDtypeStruct(store_k.shape, store_k.dtype),
            jax.ShapeDtypeStruct(store_v.shape, store_v.dtype),
        ),
        scratch_shapes=[pltpu.SemaphoreType.DMA((2,))],
        compiler_params=pltpu.CompilerParams(vmem_limit_bytes=16 << 20),
        name="write",
    )(store_k, store_v)


def per_device(
    prefill_q, cache_k, cache_v, page_counts, page_owner, decode_q, decode_k, decode_v, context_len
):
    n = lax.axis_size("seq")
    me = lax.axis_index("seq")
    page_slots = cache_k.shape[0] // PAGE
    cap = max(2, 2 * page_slots // n)
    ck = cache_k.reshape(page_slots, PAGE, KVD)
    cv = cache_v.reshape(page_slots, PAGE, KVD)
    pk, pv, meta = pack(n, cap, page_owner[:, 0], page_counts, context_len, ck, cv)
    q = jnp.concatenate((prefill_q, decode_q[0]), axis=0)
    q = q.reshape(1 + STEPS, KVH, GROUP, HD).transpose(1, 0, 2, 3).reshape(KVH, ROWS, HD)
    out, store_k, store_v, meta = main(
        n, cap, page_counts, q, meta, cache_k, cache_v, pk, pv, decode_k[0], decode_v[0]
    )
    store_k, store_v = write(store_k, store_v)
    store_k, store_v, out, meta = lax.optimization_barrier((store_k, store_v, out, meta))
    out = out.reshape(KVH, 1 + STEPS, GROUP, HD).transpose(1, 0, 2, 3).reshape(1 + STEPS, HQ * HD)
    return (
        out[:1],
        out[1:].reshape(1, STEPS, HQ * HD),
        store_k.reshape(-1, KVD),
        store_v.reshape(-1, KVD),
        meta[:, :cap, ID_LANE].reshape(-1),
    )


def solution(mesh):
    both = ("groups", "seq")
    in_specs = (
        P(both, None),
        P(both, None),
        P(both, None),
        P("groups"),
        P(both, None),
        P(both, None, None),
        P(both, None, None),
        P(both, None, None),
        P(both),
    )
    out_specs = (
        P(both, None),
        P(both, None, None),
        P(both, None),
        P(both, None),
        P(both),
    )
    return jax.shard_map(
        per_device, mesh=mesh, in_specs=in_specs, out_specs=out_specs, check_vma=False
    )
```
